32 devices in a mesh: shard: 4 (over z), ctx: 4 (over x, core), tp: 2 (over y).
Axes of the slice: x: 2, y: 2, z: 4, core: 2. Of those that a mesh axis runs over, the one named last changes fastest.
Arguments:
- layer_in: bfloat16 [3072, 2048], P(('shard', 'ctx')), may hold values from -6 to 6
- w_qkv: bfloat16 [6144, 2048], P(('shard', 'ctx'), 'tp'), may hold values from -0.125 to 0.125
- w_out: bfloat16 [2048, 2048], P(('shard', 'ctx'), 'tp'), may hold values from -1.5 to 1.5
- norm_gains: bfloat16 [2048, 4], P(('shard', 'ctx')), may hold values from 0.25 to 1.75
- router: bfloat16 [2048, 16], P(('shard', 'ctx')), may hold values from -0.0625 to 0.0625
- w_gate_up: bfloat16 [16, 2048, 2, 1024], P(('shard', 'ctx'), None, None, 'tp'), may hold values from -0.125 to 0.125
- w_down: bfloat16 [16, 2048, 1024], P(('shard', 'ctx'), None, 'tp'), may hold values from -0.75 to 0.75
- routes: int32 [3072, 8], P(('shard', 'ctx')), may hold values from 0 to 15, all different within a row; in each aligned block of 192 rows (0 to 191, 192 to 383, ...) at most 120 rows name the same one
- lengths: int32 [4, 3], P('shard'), may hold values from 1 to 614, 768 in all within a row
- token_order: int32 [4, 768], P('shard'), may hold values from 0 to 767, each once within a row
- out_grad: bfloat16 [3072, 2048], P(('shard', 'ctx')), may hold values from -6 to 6
Outputs:
- output: bfloat16 [3072, 2048], P(('shard', 'ctx'))
- input_grad: float32 [3072, 2048], P(('shard', 'ctx'))
- qkv_grad: float32 [6144, 2048], P(('shard', 'ctx'), 'tp')
- out_proj_grad: float32 [2048, 2048], P(('shard', 'ctx'), 'tp')
- gains_grad: float32 [2048, 4], P(('shard', 'ctx'))
- router_grad: float32 [2048, 16], P(('shard', 'ctx'))
- gate_up_grad: float32 [16, 2048, 2, 1024], P(('shard', 'ctx'), None, None, 'tp')
- down_grad: float32 [16, 2048, 1024], P(('shard', 'ctx'), None, 'tp')
The draws below stay inside these ranges and needn't reach their ends.
Inputs may be any that keep to these rules, and one draw needn't show every extreme that they name: `routes`: each row names 8 different experts. Among the 192 rows of one device no expert is named more than 120 times, a bound that some block reaches there. Each row holds the lengths of the 3 sequences of one group; they sum to 768 and the longest is exactly 614. `token_order`: each row is a permutation of the places of its group.
All inputs are finite; a program needn't handle non-finite values.
Results may differ from the reference program's by a relative error of at most 0.017.
Values may be sent and summed in bfloat16 or wider, within the bound.
No kernel may reach another device: no remote copies, remote signals or barrier semaphores. Data moves between devices by JAX's collectives and lax.ppermute only.
A program may use at most 320 MiB of HBM per device.

```python
import math
import jax
import jax.numpy as jnp
import numpy as np
from jax import lax

D = 2048
HEADS = 16
HEAD = 128
FF = 1024
TOPK = 8
NSEQ = 3
TOK_DEV = 192
EXPERTS = 16
CAP = 120
GROUP = 768
SEQ_MAX = 614
TOKENS = 3072
N_SHARD = 4
N_CTX = 4


def levels(own_key, dims, cuts, smallest, top_value):
    level, own = 1.0, jax.random.fold_in(own_key, 6)
    for position, shards_of in cuts:
        steps = jnp.exp(jax.random.uniform(jax.random.fold_in(own, position), (shards_of,), jnp.float32, smallest / len(cuts), top_value / len(cuts)))
        level = level * jnp.repeat(steps, dims[position] // shards_of).reshape([-1 if axis == position else 1 for axis in range(len(dims))])
    return level


def profile(number_of, total, reach, lean):
    portions = [(1 << 20) // math.isqrt(grade ** lean) + 1 for grade in range(2, number_of + 1)]
    spare, given = total - reach - (number_of - 1), [1] * (number_of - 1)
    while spare > 0:
        free = [i for i in range(number_of - 1) if given[i] < reach]
        mass, budget = sum([portions[i] for i in free]), spare
        for i in free:
            addition = min(reach - given[i], max(1, budget * portions[i] // mass), spare)
            given[i] = given[i] + addition
            spare = spare - addition
    return np.array([reach] + given)


def ragged_sizes(stream_key, count, total, bound, lean):
    if count == 2:
        one = jax.random.randint(stream_key, (), max(1, total - bound), min(bound, total - 1) + 1)
        return jnp.stack([one, total - one])
    sizes = jnp.asarray(profile(count, total, bound, lean), jnp.int32)
    couples = (count - 1) // 2
    donor, receiver = sizes[1:1 + 2 * couples:2], sizes[2:2 + 2 * couples:2]
    room = jnp.minimum(donor - 1, bound - receiver)
    moved = jax.random.randint(jax.random.fold_in(stream_key, 1), (couples,), 0, 1 << 20) % (room + 1)
    sizes = sizes.at[1:1 + 2 * couples:2].set(donor - moved).at[2:2 + 2 * couples:2].set(receiver + moved)
    return sizes[jax.random.permutation(jax.random.fold_in(stream_key, 2), count)]


def deal_out(rng, own, number, rows, count, top, reach, slope):
    ranking = jax.random.permutation(rng, count)
    heavy_load, usual = shares(count, rows * top, reach, slope, True), shares(count, rows * top, reach, slope, False)
    places = jnp.arange(count)

    def named(sizes, turn):
        used = int((sizes > 0).sum())
        fixed = max(1, used // 4)
        moved = fixed + (places - fixed + turn * (used - fixed)) % max(1, count - fixed)
        return jnp.zeros((count,), jnp.int32).at[ranking[jnp.where(places < fixed, places, moved)]].set(jnp.asarray(sizes, jnp.int32))

    sizes = jnp.where(number % 4 == 0, named(heavy_load, number // 4), named(usual, number - number // 4 - 1))
    mixed = jax.random.permutation(jax.random.fold_in(own, 3), count)
    giver, taker = mixed[0:count // 2 * 2:2], mixed[1:count // 2 * 2:2]
    room = jnp.minimum(sizes[giver] - 1, reach - sizes[taker]) // 2
    room = jnp.where((giver == ranking[0]) | (taker == ranking[0]) | (sizes[taker] == 0), 0, jnp.maximum(room, 0))
    moved = jax.random.randint(jax.random.fold_in(own, 4), (count // 2,), 0, 1 << 20) % (room + 1)
    sizes = sizes.at[giver].add(-moved).at[taker].add(moved)
    items = jnp.searchsorted(jnp.cumsum(sizes), jnp.arange(rows * top), side="right").astype(jnp.int32)
    table = items.reshape(top, rows).T
    table = table[jax.random.permutation(jax.random.fold_in(own, 1), rows)]
    turn = jax.random.randint(jax.random.fold_in(own, 2), (rows, 1), 0, top)
    return jnp.take_along_axis(table, (jnp.arange(top)[None, :] + turn) % top, axis=1)


def shares(count, total, bound, lean, full):
    loads = [(1 << 20) // math.isqrt(rank ** lean) + 1 for rank in range(1, count + 1)]
    largest = bound if full else min(bound, max(-(-total // count), total * loads[0] // sum(loads)))
    least = 1 if total - largest >= count - 1 else 0
    holding, rest = [largest] + [least] * (count - 1), total - largest - least * (count - 1)
    while rest > 0:
        movable = [i for i in range(1, count) if holding[i] < largest] or [i for i in range(1, count) if holding[i] < bound]
        mass, left = sum([loads[i] for i in movable]), rest
        for i in movable:
            more = min(bound - holding[i], max(1, left * loads[i] // mass), rest)
            holding[i] = holding[i] + more
            rest = rest - more
    return np.array(holding)


def normal_values(own_key, shape, scale, most, split=(), kind=jnp.bfloat16):
    values = jax.random.normal(own_key, shape, jnp.float32) * scale
    if len(split) > 0:
        values = levels(own_key, shape, split, -0.22, 0.18) * values
    return jnp.clip(values, min=-most, max=most).astype(kind)


def setup_inputs(seed: int = 0) -> dict:
    splits = jax.random.split(jax.random.key(seed), 12)
    layer_in = normal_values(splits[0], (TOKENS, D), 1.0, 6.0, ((0, 16),))
    w_qkv = normal_values(splits[1], (3 * D, HEADS * HEAD), D ** -0.5, 0.125, ((0, 16), (1, 2)))
    w_out = normal_values(splits[2], (D, HEADS * HEAD), (max(HEADS * HEAD // 128, 1)) ** -0.5, 1.5, ((0, 16), (1, 2)))
    norm_gains = jnp.clip(1.0 + 0.15 * jax.random.normal(splits[3], (D, 4), jnp.float32), 0.25, 1.75).astype(jnp.bfloat16)
    router = normal_values(splits[4], (D, EXPERTS), (4 * D) ** -0.5, 0.0625, ((0, 16),))
    w_gate_up = normal_values(splits[5], (EXPERTS, D, 2, FF), D ** -0.5, 0.125, ((0, 16), (3, 2)))
    w_down = normal_values(splits[6], (EXPERTS, D, FF), (max(FF // 16, 1)) ** -0.5, 0.75, ((0, 16), (2, 2)))
    routes_keys = jax.random.split(jax.random.fold_in(splits[7], 1), TOKENS // TOK_DEV)
    routes_turns = jax.random.permutation(jax.random.fold_in(splits[7], 3), TOKENS // TOK_DEV)
    routes = jax.vmap(lambda own, number: deal_out(jax.random.fold_in(splits[7], 2), own, number, TOK_DEV, EXPERTS, TOPK, CAP, 2))(routes_keys, routes_turns).reshape((TOKENS, TOPK))
    lengths = jax.vmap(lambda own: ragged_sizes(own, NSEQ, GROUP, SEQ_MAX, 2))(jax.random.split(splits[8], N_SHARD)).reshape((N_SHARD, NSEQ)).astype(jnp.int32)
    token_order = jax.vmap(lambda own: jax.random.permutation(own, GROUP))(jax.random.split(splits[9], N_SHARD)).reshape((N_SHARD, GROUP)).astype(jnp.int32)
    out_grad = normal_values(splits[10], (TOKENS, D), 1.0, 6.0, ((0, 16),))
    return {"layer_in": layer_in, "w_qkv": w_qkv, "w_out": w_out, "norm_gains": norm_gains, "router": router, "w_gate_up": w_gate_up, "w_down": w_down, "routes": routes, "lengths": lengths, "token_order": token_order, "out_grad": out_grad}


@jax.custom_vjp
def low(v):
    return lax.optimization_barrier(v.astype(jnp.bfloat16)).astype(jnp.float32)

@jax.custom_vjp
def low_back(v):
    return v

def low_keep(v):
    return (low(v), None)

def low_pass(kept, grad):
    return (grad,)

def back_keep(v):
    return (v, None)

def back_low(kept, grad):
    return (low(grad),)
low.defvjp(low_keep, low_pass)
low_back.defvjp(back_keep, back_low)
norm_eps = 1e-05
rope_base = 10000.0
masked_score = -1e+30

def places_info(order_row, length_row):
    seq_ends = jnp.cumsum(length_row).astype(jnp.int32)
    seq_starts = (seq_ends - length_row).astype(jnp.int32)
    sequence = lax.optimization_barrier(jnp.sum((order_row[:, None] >= seq_ends[None, :]).astype(jnp.int32), axis=1)).astype(jnp.int32)
    picker = jnp.arange(length_row.shape[0], dtype=jnp.int32)[None, :] == sequence[:, None]
    first_place = lax.optimization_barrier(jnp.sum(jnp.where(picker, seq_starts[None, :], 0), axis=1)).astype(jnp.int32)
    return (sequence, (order_row - first_place).astype(jnp.int32))

def rope_tables(place_pos, head_size):
    freq_index = jnp.arange(head_size // 2, dtype=jnp.float32)
    inverse = 1.0 / rope_base ** (freq_index * 2.0 / head_size)
    angle = place_pos.astype(jnp.float32)[:, None] * inverse[None, :]
    cosine = jnp.cos(angle)
    sine = jnp.sin(angle)
    return (jnp.concatenate([cosine, cosine], 1), jnp.concatenate([sine, sine], 1))

def rotate(values_in, cosine, sine):
    half_width = values_in.shape[-1] // 2
    turned = jnp.concatenate([-values_in[..., half_width:], values_in[..., :half_width]], -1)
    return values_in * cosine[:, None, :] + turned * sine[:, None, :]

def rms_rows(values_in):
    return values_in * lax.rsqrt(lax.optimization_barrier(jnp.mean(values_in * values_in, axis=-1, keepdims=True)) + norm_eps)

def softmax_last(scores):
    row_max = lax.optimization_barrier(jnp.max(scores, axis=-1, keepdims=True))
    shifted = jnp.exp(scores - row_max)
    return shifted / lax.optimization_barrier(jnp.sum(shifted, axis=-1, keepdims=True))

def slot_index(expert_flat, expert_count, capacity):
    chosen = (expert_flat[:, None] == jnp.arange(expert_count, dtype=jnp.int32)[None, :]).astype(jnp.int32)
    before = jnp.cumsum(chosen, axis=0).astype(jnp.int32) - chosen
    slot_num = lax.optimization_barrier(jnp.sum(before * chosen, axis=1)).astype(jnp.int32)
    return (expert_flat * capacity + slot_num).astype(jnp.int32)

def reference(layer_in, w_qkv, w_out, norm_gains, router, w_gate_up, w_down, routes, lengths, token_order, out_grad):
    blocks = N_SHARD * N_CTX
    group_len = TOK_DEV * N_CTX
    full_heads = HEADS * HEAD
    score_scale = HEAD ** (-0.5)
    highest = lax.Precision.HIGHEST
    seq_ids, positions = jax.vmap(places_info)(token_order, lengths)
    cosine, sine = rope_tables(positions.reshape(-1), HEAD)

    def block_slots(route_row):
        return slot_index(route_row, EXPERTS, CAP)
    slot_dest = jax.vmap(block_slots)(routes.reshape(blocks, TOK_DEV * TOPK))
    token_of = (jnp.arange(TOK_DEV * TOPK, dtype=jnp.int32) // TOPK).astype(jnp.int32)

    def forward(layer_f, qkv_f, out_f, gains_f, router_f, gate_up_f, down_f):

        def attend(group_in):
            query_g, key_g, value_g, seq_g, pos_g = group_in
            visible = (seq_g[:, None] == seq_g[None, :]) & (pos_g[None, :] <= pos_g[:, None])
            scores = low_back(jnp.einsum('qhd,khd->hqk', query_g, key_g, precision=highest) * score_scale)
            scores = jnp.where(visible[None], scores, masked_score)
            weights = low(softmax_last(scores))
            return jnp.einsum('hqk,khd->qhd', weights, value_g, precision=highest)

        def expert_block(block_in):
            rows_b, gates_b, dest_b = block_in
            slots = jnp.zeros((EXPERTS * CAP, D), rows_b.dtype).at[dest_b].set(rows_b[token_of])
            slots = slots.reshape(EXPERTS, CAP, D)
            gate_up = low_back(jnp.einsum('ecd,edjf->ecjf', slots, gate_up_f, precision=highest))
            gate_val = gate_up[:, :, 0]
            hidden_act = low(gate_val * jax.nn.sigmoid(gate_val) * gate_up[:, :, 1])
            result = low_back(jnp.einsum('ecf,edf->ecd', hidden_act, down_f, precision=highest))
            picked_rows = result.reshape(EXPERTS * CAP, D)[dest_b].reshape(TOK_DEV, TOPK, D)
            return lax.optimization_barrier(jnp.sum(gates_b[:, :, None] * picked_rows, axis=1))
        normed = rms_rows(layer_f) * gains_f[:, 0]
        normed_low = low(normed)
        projected = low_back(jnp.einsum('td,jdh->tjh', normed_low, qkv_f.reshape(3, D, full_heads), precision=highest))
        query = rms_rows(projected[:, 0]) * gains_f[:, 2]
        keyed = rms_rows(projected[:, 1]) * gains_f[:, 3]
        valued = low(projected[:, 2]).reshape(N_SHARD, group_len, HEADS, HEAD)
        query = low(rotate(query.reshape(TOKENS, HEADS, HEAD), cosine, sine)).reshape(N_SHARD, group_len, HEADS, HEAD)
        keyed = low(rotate(keyed.reshape(TOKENS, HEADS, HEAD), cosine, sine)).reshape(N_SHARD, group_len, HEADS, HEAD)
        mixed = lax.map(jax.checkpoint(attend), (query, keyed, valued, seq_ids, positions))
        mixed = low_back(low(mixed.reshape(TOKENS, full_heads)))
        attn = low_back(jnp.dot(mixed, out_f.T, precision=highest))
        resid = layer_f + attn
        middle = rms_rows(resid) * gains_f[:, 1]
        middle_low = low(middle)
        logits = jnp.dot(middle, router_f, precision=highest)
        gates = softmax_last(jnp.take_along_axis(logits, routes, axis=1))
        mixture = lax.map(jax.checkpoint(expert_block), (middle_low.reshape(blocks, TOK_DEV, D), gates.reshape(blocks, TOK_DEV, TOPK), slot_dest))
        return resid + mixture.reshape(TOKENS, D)
    float_args = tuple((item.astype(jnp.float32) for item in (layer_in, w_qkv, w_out, norm_gains, router, w_gate_up, w_down)))
    result_out, pullback = jax.vjp(forward, *float_args)
    gradients = pullback(out_grad.astype(jnp.float32))
    return (result_out.astype(jnp.bfloat16), gradients[0], gradients[1], gradients[2], gradients[3], gradients[4], gradients[5], gradients[6])
```

```python
import jax
import jax.numpy as jnp
from jax import lax
from jax.sharding import PartitionSpec as P

HEAD = 128
LANES = 128


norm_eps = 1e-05
rope_base = 10000.0
masked_score = -1e30


def places_info(order_row, length_row):
    seq_ends = jnp.cumsum(length_row)
    seq_starts = seq_ends - length_row
    sequence = jnp.sum((order_row[:, None] >= seq_ends[None, :]).astype(jnp.int32), axis=1)
    picker = jnp.arange(length_row.shape[0], dtype=jnp.int32)[None, :] == sequence[:, None]
    first_place = jnp.sum(jnp.where(picker, seq_starts[None, :], 0), axis=1)
    return (sequence, order_row - first_place)


def rope_tables(place_pos, head_size):
    freq_index = jnp.arange(head_size // 2, dtype=jnp.float32)
    inverse = 1.0 / rope_base ** (freq_index * 2.0 / head_size)
    angle = place_pos.astype(jnp.float32)[:, None] * inverse[None, :]
    cosine = jnp.cos(angle)
    sine = jnp.sin(angle)
    return (jnp.concatenate([cosine, cosine], 1), jnp.concatenate([sine, sine], 1))


def rotate(values_in, cosine, sine):
    half_width = values_in.shape[-1] // 2
    turned = jnp.concatenate([-values_in[..., half_width:], values_in[..., :half_width]], -1)
    return values_in * cosine[:, None, :] + turned * sine[:, None, :]


def rotate_back(grad_in, cosine, sine):
    half_width = grad_in.shape[-1] // 2
    scaled = grad_in * sine[:, None, :]
    return grad_in * cosine[:, None, :] + jnp.concatenate(
        [scaled[..., half_width:], -scaled[..., :half_width]], -1
    )


def swap_tp(values_in):
    return lax.ppermute(values_in, "tp", [(0, 1), (1, 0)])


def swap_ctx(values_in, bit):
    return lax.ppermute(values_in, "ctx", [(i, i ^ bit) for i in range(lax.axis_size("ctx"))])


def join_halves(mine, other, first_is_mine):
    top = jnp.where(first_is_mine, mine, other)
    bottom = jnp.where(first_is_mine, other, mine)
    return jnp.concatenate([top, bottom], axis=0)


def split_three(values_in):
    high = values_in.astype(jnp.bfloat16)
    rest = values_in - high.astype(jnp.float32)
    middle = rest.astype(jnp.bfloat16)
    low = (rest - middle.astype(jnp.float32)).astype(jnp.bfloat16)
    return [high, middle, low]


def local(
    layer_in,
    w_qkv,
    w_out,
    norm_gains,
    router,
    w_gate_up,
    w_down,
    routes,
    lengths,
    token_order,
    out_grad,
):
    bf16, f32 = jnp.bfloat16, jnp.float32
    highest = lax.Precision.HIGHEST
    tokens, width = layer_in.shape
    experts = router.shape[1]
    hidden = w_down.shape[2]
    half = tokens // 2
    owners = ("shard", "ctx")
    tp_index = lax.axis_index("tp")
    ctx_index = lax.axis_index("ctx")
    ctx_size = lax.axis_size("ctx")
    expert_index = lax.axis_index("shard") * ctx_size + ctx_index
    first_is_mine = tp_index == 0
    my_row = tp_index * half
    other_row = (1 - tp_index) * half

    def my_rows(values_in):
        return lax.dynamic_slice_in_dim(values_in, my_row, half)

    def other_rows(values_in):
        return lax.dynamic_slice_in_dim(values_in, other_row, half)

    small_all = lax.all_gather(
        jnp.concatenate([norm_gains, router], axis=1), owners, axis=0, tiled=True
    )
    qkv_all = lax.all_gather(w_qkv, owners, axis=0, tiled=True)
    out_all = lax.all_gather(w_out, owners, axis=0, tiled=True)
    grad_half = my_rows(out_grad)
    grad_rows = lax.all_gather(grad_half, owners, axis=0, tiled=True)
    gate_own = w_gate_up[0, :, 0]
    up_own = w_gate_up[0, :, 1]
    down_own = w_down[0]
    gate_other, up_other, down_other = swap_tp(gate_own), swap_tp(up_own), swap_tp(down_own)
    w_in = jnp.concatenate([gate_own, gate_other, up_own, up_other], axis=1)
    w_back = jnp.concatenate([down_own, down_other], axis=1)

    half_width = qkv_all.shape[1]
    full_heads = half_width * lax.axis_size("tp")
    head_count = half_width // HEAD
    gains_f = small_all[:, :4].astype(f32)
    router_f = small_all[:, 4:].astype(f32)
    gain_in = gains_f[:, 0]
    gain_mid = gains_f[:, 1]
    gain_q = lax.dynamic_slice_in_dim(gains_f[:, 2], tp_index * half_width, half_width)
    gain_k = lax.dynamic_slice_in_dim(gains_f[:, 3], tp_index * half_width, half_width)
    score_scale = HEAD ** (-0.5)
    seq_all, pos_all = places_info(token_order[0], lengths[0])

    def ctx_rows(table, index):
        return lax.dynamic_slice_in_dim(table, index * tokens, tokens)

    seq_mine, pos_mine = ctx_rows(seq_all, ctx_index), ctx_rows(pos_all, ctx_index)
    key_order = [ctx_index ^ step for step in range(ctx_size)]
    seq_keys = jnp.concatenate([ctx_rows(seq_all, i) for i in key_order])
    pos_keys = jnp.concatenate([ctx_rows(pos_all, i) for i in key_order])
    cosine, sine = rope_tables(pos_mine, HEAD)
    visible = (seq_mine[:, None] == seq_keys[None, :]) & (pos_keys[None, :] <= pos_mine[:, None])

    layer_f = layer_in.astype(f32)
    rate_in = lax.rsqrt(jnp.mean(layer_f * layer_f, axis=-1, keepdims=True) + norm_eps)
    in_hat = layer_f * rate_in
    in_low = (in_hat * gain_in).astype(bf16)
    qkv_mats = qkv_all.reshape(3, width, half_width)
    q_raw, k_raw, v_raw = (
        jnp.dot(in_low, qkv_mats[j], preferred_element_type=f32) for j in range(3)
    )
    square_q, square_k = lax.psum(
        (jnp.sum(q_raw * q_raw, axis=1), jnp.sum(k_raw * k_raw, axis=1)), "tp"
    )
    rate_q = lax.rsqrt(square_q / full_heads + norm_eps)[:, None]
    rate_k = lax.rsqrt(square_k / full_heads + norm_eps)[:, None]
    q_hat = q_raw * rate_q
    k_hat = k_raw * rate_k
    q_low = rotate((q_hat * gain_q).reshape(tokens, head_count, HEAD), cosine, sine).astype(bf16)
    k_low = (
        rotate((k_hat * gain_k).reshape(tokens, head_count, HEAD), cosine, sine)
        .astype(bf16)
        .reshape(tokens, half_width)
    )
    v_low = v_raw.astype(bf16)

    def gather_ctx(block):
        far = swap_ctx(block, 2)
        return jnp.concatenate([block, swap_ctx(block, 1), far, swap_ctx(far, 1)], axis=0)

    group_len = tokens * ctx_size
    key_heads = gather_ctx(k_low).reshape(group_len, head_count, HEAD)
    value_heads = gather_ctx(v_low).reshape(group_len, head_count, HEAD)
    scores = jnp.einsum("qhd,khd->hqk", q_low, key_heads, preferred_element_type=f32) * score_scale
    scores = jnp.where(visible[None], scores, masked_score)
    row_max = jnp.max(scores, axis=-1, keepdims=True)
    shifted = jnp.exp(scores - row_max)
    row_sum = jnp.sum(shifted, axis=-1, keepdims=True)
    weights = shifted / row_sum
    log_total = row_max + jnp.log(row_sum)
    mixed = jnp.einsum(
        "hqk,khd->qhd", weights.astype(bf16), value_heads, preferred_element_type=f32
    )
    mixed_low = mixed.reshape(tokens, half_width).astype(bf16)
    attn_part = lax.dot_general(
        mixed_low, out_all, (((1,), (1,)), ((), ())), preferred_element_type=f32
    )
    attn = my_rows(attn_part) + swap_tp(other_rows(attn_part).astype(bf16)).astype(f32)

    resid = my_rows(layer_f) + attn
    rate_mid = lax.rsqrt(jnp.mean(resid * resid, axis=-1, keepdims=True) + norm_eps)
    mid_hat = resid * rate_mid
    mid_norm = mid_hat * gain_mid
    logits = jnp.dot(mid_norm, router_f, precision=highest)
    expert_ids = jnp.arange(experts, dtype=jnp.int32)
    chosen = jnp.any(my_rows(routes)[:, :, None] == expert_ids[None, None, :], axis=1)
    logits_max = jnp.max(jnp.where(chosen, logits, -jnp.inf), axis=-1, keepdims=True)
    gates = jnp.where(chosen, jnp.exp(jnp.where(chosen, logits - logits_max, 0.0)), 0.0)
    gates = gates / jnp.sum(gates, axis=-1, keepdims=True)

    def padded(parts):
        columns = sum(part.shape[1] for part in parts)
        rest = -columns % LANES
        if rest:
            parts = parts + [jnp.zeros((parts[0].shape[0], rest), parts[0].dtype)]
        return jnp.concatenate(parts, axis=1)

    mid_rows = lax.all_gather(
        padded([mid_norm.astype(bf16)] + split_three(gates)), owners, axis=0, tiled=True
    )
    extra = mid_rows[:, width:].astype(f32)
    column = jnp.arange(extra.shape[1], dtype=jnp.int32)
    mine_in = (column % experts == expert_index) & (column < 3 * experts)
    gate_col = jnp.sum(jnp.where(mine_in[None, :], extra, 0.0), axis=1, keepdims=True)
    mid_all = mid_rows[:, :width]

    hidden_raw = jnp.dot(grad_rows, w_back, preferred_element_type=f32)
    both = jnp.dot(mid_all, w_in, preferred_element_type=f32)
    gate_val, up_val = both[:, : 2 * hidden], both[:, 2 * hidden :]
    gate_sig = jax.nn.sigmoid(gate_val)
    gate_act = gate_val * gate_sig
    hidden_act = gate_act * up_val
    score_col = jnp.sum(hidden_act * hidden_raw, axis=1, keepdims=True)
    gated_act = (gate_col * hidden_act).astype(bf16)
    hidden_grad = gate_col * hidden_raw
    gate_grad = hidden_grad * up_val * gate_sig * (1.0 + gate_val * (1.0 - gate_sig))
    up_grad = hidden_grad * gate_act
    both_grad = jnp.concatenate([gate_grad.astype(bf16), up_grad.astype(bf16)], axis=1)
    mix_part = lax.dot_general(
        gated_act, w_back, (((1,), (1,)), ((), ())), preferred_element_type=f32
    ).astype(bf16)
    back_part = lax.dot_general(
        both_grad, w_in, (((1,), (1,)), ((), ())), preferred_element_type=f32
    ).astype(bf16)
    score_high = score_col.astype(bf16)
    score_low = (score_col - score_high.astype(f32)).astype(bf16)
    pads = -2 * experts % LANES + 2 * experts
    spot = jnp.arange(pads, dtype=jnp.int32)[None, :]
    zero = jnp.zeros((), bf16)
    score_part = jnp.where(
        spot == expert_index, score_high, jnp.where(spot == expert_index + experts, score_low, zero)
    )
    mix_sum = lax.psum_scatter(
        jnp.concatenate([mix_part, score_part], axis=1), owners, scatter_dimension=0, tiled=True
    )
    back_sum = lax.psum_scatter(back_part, owners, scatter_dimension=0, tiled=True)

    in_grad = lax.dot_general(
        mid_all, both_grad, (((0,), (0,)), ((), ())), preferred_element_type=f32
    )
    back_grad = lax.dot_general(
        grad_rows, gated_act, (((0,), (0,)), ((), ())), preferred_element_type=f32
    )

    def own_total(total, index):
        own = total[:, 2 * index * hidden : (2 * index + 1) * hidden]
        other = total[:, (2 * index + 1) * hidden : (2 * index + 2) * hidden]
        return own + swap_tp(other.astype(bf16)).astype(f32)

    gate_up_grad = jnp.stack([own_total(in_grad, 0), own_total(in_grad, 1)], axis=1)[None]
    down_grad = own_total(back_grad, 0)[None]

    mixture = mix_sum[:, :width].astype(f32)
    score_total = (
        mix_sum[:, width : width + experts].astype(f32)
        + mix_sum[:, width + experts : width + 2 * experts].astype(f32)
    )
    mid_grad = back_sum.astype(f32)
    output_half = (resid + mixture).astype(bf16)
    output = join_halves(output_half, swap_tp(output_half), first_is_mine)
    logit_grad = gates * (score_total - jnp.sum(gates * score_total, axis=1, keepdims=True))
    router_grad = lax.dot_general(
        logit_grad, mid_norm, (((0,), (0,)), ((), ())), precision=highest
    )
    mid_grad = mid_grad + lax.dot_general(
        logit_grad, router_f, (((1,), (1,)), ((), ())), precision=highest
    )
    mid_scaled = gain_mid * mid_grad
    resid_grad = grad_half.astype(f32) + rate_mid * (
        mid_scaled - mid_hat * jnp.mean(mid_hat * mid_scaled, axis=-1, keepdims=True)
    )
    gain_mid_grad = jnp.sum(mid_grad * mid_hat, axis=0, keepdims=True)
    attn_half = resid_grad.astype(bf16)
    attn_low = join_halves(attn_half, swap_tp(attn_half), first_is_mine)
    out_proj_grad = lax.dot_general(
        attn_low, mixed_low, (((0,), (0,)), ((), ())), preferred_element_type=f32
    ).astype(bf16)
    out_owned = lax.psum_scatter(
        out_proj_grad, owners, scatter_dimension=0, tiled=True
    ).astype(f32)
    mixed_grad = (
        jnp.dot(attn_low, out_all, preferred_element_type=f32)
        .astype(bf16)
        .reshape(tokens, head_count, HEAD)
    )
    again = jnp.einsum("qhd,khd->hqk", q_low, key_heads, preferred_element_type=f32) * score_scale
    again = jnp.where(visible[None], again, masked_score)
    weights_again = jnp.exp(again - log_total)
    weights_low = weights_again.astype(bf16)
    weight_grad = jnp.einsum("qhd,khd->hqk", mixed_grad, value_heads, preferred_element_type=f32)
    score_grad = weights_again * (
        weight_grad - jnp.sum(weights_again * weight_grad, axis=-1, keepdims=True)
    )
    score_low = score_grad.astype(bf16)
    q_grad = (
        jnp.einsum("hqk,khd->qhd", score_low, key_heads, preferred_element_type=f32) * score_scale
    )
    k_part = (
        jnp.einsum("hqk,qhd->khd", score_low, q_low, preferred_element_type=f32) * score_scale
    )
    v_part = jnp.einsum("hqk,qhd->khd", weights_low, mixed_grad, preferred_element_type=f32)

    def scatter_ctx(part):
        part = part.reshape(ctx_size, tokens, half_width)
        near = part[0] + swap_ctx(part[1].astype(bf16), 1).astype(f32)
        far = part[2] + swap_ctx(part[3].astype(bf16), 1).astype(f32)
        return near + swap_ctx(far.astype(bf16), 2).astype(f32)

    k_grad, v_grad = scatter_ctx(k_part), scatter_ctx(v_part)
    q_in = rotate_back(q_grad, cosine, sine).reshape(tokens, half_width)
    k_in = rotate_back(k_grad.reshape(tokens, head_count, HEAD), cosine, sine).reshape(
        tokens, half_width
    )
    q_scaled = gain_q * q_in
    k_scaled = gain_k * k_in
    inner_q, inner_k = lax.psum(
        (jnp.sum(q_scaled * q_hat, axis=1), jnp.sum(k_scaled * k_hat, axis=1)), "tp"
    )
    q_raw_grad = rate_q * (q_scaled - q_hat * (inner_q / full_heads)[:, None])
    k_raw_grad = rate_k * (k_scaled - k_hat * (inner_k / full_heads)[:, None])
    raw_grads = [q_raw_grad.astype(bf16), k_raw_grad.astype(bf16), v_grad.astype(bf16)]
    qkv_grad = jnp.concatenate(
        [
            lax.dot_general(
                in_low, raw, (((0,), (0,)), ((), ())), preferred_element_type=f32
            ).astype(bf16)
            for raw in raw_grads
        ],
        axis=0,
    )
    qkv_owned = lax.psum_scatter(qkv_grad, owners, scatter_dimension=0, tiled=True).astype(f32)
    norm_part = sum(
        lax.dot_general(raw, mat, (((1,), (1,)), ((), ())), preferred_element_type=f32)
        for raw, mat in zip(raw_grads, (qkv_mats[0], qkv_mats[1], qkv_mats[2]))
    )
    in_norm_grad = my_rows(norm_part) + swap_tp(other_rows(norm_part).astype(bf16)).astype(f32)
    in_hat_half = my_rows(in_hat)
    in_scaled = gain_in * in_norm_grad
    input_half = resid_grad + my_rows(rate_in) * (
        in_scaled - in_hat_half * jnp.mean(in_hat_half * in_scaled, axis=-1, keepdims=True)
    )
    input_grad = join_halves(input_half, swap_tp(input_half), first_is_mine)
    gain_in_grad = jnp.sum(in_norm_grad * in_hat_half, axis=0, keepdims=True)
    gain_pair = jnp.stack([jnp.sum(q_in * q_hat, axis=0), jnp.sum(k_in * k_hat, axis=0)], axis=0)
    qk_gain_part = lax.dynamic_update_slice(
        jnp.zeros((2, width), f32), gain_pair, (0, tp_index * half_width)
    )
    everyone = ("shard", "ctx", "tp")
    router_total = lax.psum(router_grad, everyone)
    gains_total = lax.psum(
        jnp.concatenate([gain_in_grad, gain_mid_grad, qk_gain_part], axis=0), everyone
    )
    own_rows = norm_gains.shape[0]

    def owned(total):
        return lax.dynamic_slice_in_dim(total, expert_index * own_rows, own_rows, axis=1).T

    return (
        output,
        input_grad,
        qkv_owned,
        out_owned,
        owned(gains_total),
        owned(router_total),
        gate_up_grad,
        down_grad,
    )


def solution(mesh):
    in_specs = (
        P(("shard", "ctx"), None),
        P(("shard", "ctx"), "tp"),
        P(("shard", "ctx"), "tp"),
        P(("shard", "ctx"), None),
        P(("shard", "ctx"), None),
        P(("shard", "ctx"), None, None, "tp"),
        P(("shard", "ctx"), None, "tp"),
        P(("shard", "ctx"), None),
        P("shard", None),
        P("shard", None),
        P(("shard", "ctx"), None),
    )
    out_specs = (
        P(("shard", "ctx"), None),
        P(("shard", "ctx"), None),
        P(("shard", "ctx"), "tp"),
        P(("shard", "ctx"), "tp"),
        P(("shard", "ctx"), None),
        P(("shard", "ctx"), None),
        P(("shard", "ctx"), None, None, "tp"),
        P(("shard", "ctx"), None, "tp"),
    )
    return jax.shard_map(local, mesh=mesh, in_specs=in_specs, out_specs=out_specs, check_vma=False)
```

```python
import functools
import math

import jax
import jax.numpy as jnp
from jax import lax
from jax.experimental import pallas as pl
from jax.experimental.pallas import tpu as pltpu
from jax.sharding import PartitionSpec as P

HEAD = 128
LANES = 128


norm_eps = 1e-05
rope_base = 10000.0
masked_score = -1e30


def places_info(order_row, length_row):
    seq_ends = jnp.cumsum(length_row)
    seq_starts = seq_ends - length_row
    sequence = jnp.sum((order_row[:, None] >= seq_ends[None, :]).astype(jnp.int32), axis=1)
    picker = jnp.arange(length_row.shape[0], dtype=jnp.int32)[None, :] == sequence[:, None]
    first_place = jnp.sum(jnp.where(picker, seq_starts[None, :], 0), axis=1)
    return (sequence, order_row - first_place)


def rope_tables(place_pos, head_size):
    freq_index = jnp.arange(head_size // 2, dtype=jnp.float32)
    inverse = 1.0 / rope_base ** (freq_index * 2.0 / head_size)
    angle = place_pos.astype(jnp.float32)[:, None] * inverse[None, :]
    cosine = jnp.cos(angle)
    sine = jnp.sin(angle)
    return (jnp.concatenate([cosine, cosine], 1), jnp.concatenate([sine, sine], 1))


def rotate(values_in, cosine, sine):
    half_width = values_in.shape[-1] // 2
    turned = jnp.concatenate([-values_in[..., half_width:], values_in[..., :half_width]], -1)
    return values_in * cosine[:, None, :] + turned * sine[:, None, :]


def rotate_back(grad_in, cosine, sine):
    half_width = grad_in.shape[-1] // 2
    scaled = grad_in * sine[:, None, :]
    return grad_in * cosine[:, None, :] + jnp.concatenate(
        [scaled[..., half_width:], -scaled[..., :half_width]], -1
    )


def swap_tp(values_in):
    return lax.ppermute(values_in, "tp", [(0, 1), (1, 0)])


def swap_ctx(values_in, bit):
    return lax.ppermute(values_in, "ctx", [(i, i ^ bit) for i in range(lax.axis_size("ctx"))])


def shift_shard(values_in, step):
    size = lax.axis_size("shard")
    return lax.ppermute(values_in, "shard", [(i, (i + step) % size) for i in range(size)])


def sum_all(values_in):
    total = values_in + swap_tp(values_in)
    for axis in ("ctx", "shard"):
        size, bit = lax.axis_size(axis), 1
        while bit < size:
            total = total + lax.ppermute(total, axis, [(i, i ^ bit) for i in range(size)])
            bit *= 2
    return total


def add_low(first, *others):
    total = first.astype(jnp.float32)
    for other in others:
        total = total + other.astype(jnp.float32)
    return total


def weight_grad_kernel(sub, count, added, order_ref, rows_ref, raw_ref, *refs):
    out_ref = refs[-1]
    block = order_ref[pl.program_id(0)]
    pieces = out_ref.shape[1] // sub
    for piece in range(pieces):
        granule = block * pieces + piece
        matrix = granule // count
        start = pl.multiple_of((granule % count) * sub, sub)
        total = jnp.dot(
            rows_ref[pl.ds(start, sub), :], raw_ref[matrix], preferred_element_type=jnp.float32
        )
        here = slice(piece * sub, (piece + 1) * sub)
        if added:
            total = total + refs[0][0, here, :].astype(jnp.float32)
        out_ref[0, here, :] = total.astype(jnp.bfloat16)


def weight_grad_blocks(order, rows, raw, block_rows, added=None):
    width, tokens = rows.shape
    columns = raw.shape[2]
    sub = math.gcd(block_rows, width)
    blocks = order.shape[0]
    block_spec = pl.BlockSpec((1, block_rows, columns), lambda i, order: (i, 0, 0))
    in_specs = [
        pl.BlockSpec((width, tokens), lambda i, order: (0, 0)),
        pl.BlockSpec(raw.shape, lambda i, order: (0, 0, 0)),
    ]
    operands = [rows, raw]
    if added is not None:
        in_specs.append(block_spec)
        operands.append(added)
    return pl.pallas_call(
        functools.partial(weight_grad_kernel, sub, width // sub, added is not None),
        out_shape=jax.ShapeDtypeStruct((blocks, block_rows, columns), jnp.bfloat16),
        grid_spec=pltpu.PrefetchScalarGridSpec(
            num_scalar_prefetch=1,
            grid=(blocks,),
            in_specs=in_specs,
            out_specs=block_spec,
        ),
        cost_estimate=pl.CostEstimate(
            flops=2 * blocks * block_rows * tokens * columns,
            bytes_accessed=2 * blocks * block_rows * columns * len(in_specs),
            transcendentals=0,
        ),
    )(order, *operands)


def join_halves(mine, other, first_is_mine):
    top = jnp.where(first_is_mine, mine, other)
    bottom = jnp.where(first_is_mine, other, mine)
    return jnp.concatenate([top, bottom], axis=0)


def split_three(values_in):
    high = values_in.astype(jnp.bfloat16)
    rest = values_in - high.astype(jnp.float32)
    middle = rest.astype(jnp.bfloat16)
    low = (rest - middle.astype(jnp.float32)).astype(jnp.bfloat16)
    return [high, middle, low]


def local(
    layer_in,
    w_qkv,
    w_out,
    norm_gains,
    router,
    w_gate_up,
    w_down,
    routes,
    lengths,
    token_order,
    out_grad,
):
    bf16, f32 = jnp.bfloat16, jnp.float32
    highest = lax.Precision.HIGHEST
    tokens, width = layer_in.shape
    experts = router.shape[1]
    hidden = w_down.shape[2]
    half = tokens // 2
    owners = ("shard", "ctx")
    tp_index = lax.axis_index("tp")
    ctx_index = lax.axis_index("ctx")
    ctx_size = lax.axis_size("ctx")
    expert_index = lax.axis_index("shard") * ctx_size + ctx_index
    first_is_mine = tp_index == 0
    my_row = tp_index * half
    other_row = (1 - tp_index) * half

    def my_rows(values_in):
        return lax.dynamic_slice_in_dim(values_in, my_row, half)

    def other_rows(values_in):
        return lax.dynamic_slice_in_dim(values_in, other_row, half)

    small_all = lax.all_gather(
        jnp.concatenate([norm_gains, router], axis=1), owners, axis=0, tiled=True
    )
    qkv_all = lax.all_gather(w_qkv, owners, axis=0, tiled=True)
    out_all = lax.all_gather(w_out, owners, axis=0, tiled=True)
    grad_half = my_rows(out_grad)
    grad_rows = lax.all_gather(
        lax.optimization_barrier((grad_half, out_all))[0], owners, axis=0, tiled=True
    )
    own_cat = jnp.concatenate([w_gate_up[0, :, 0], w_gate_up[0, :, 1], w_down[0]], axis=1)
    with jax.named_scope("swap_weights"):
        other_cat = swap_tp(own_cat)

    def hidden_part(which, index):
        return which[:, index * hidden : (index + 1) * hidden]

    w_in = jnp.concatenate(
        [hidden_part(which, index) for index in range(2) for which in (own_cat, other_cat)], axis=1
    )
    w_back = jnp.concatenate([hidden_part(own_cat, 2), hidden_part(other_cat, 2)], axis=1)

    half_width = qkv_all.shape[1]
    full_heads = half_width * lax.axis_size("tp")
    head_count = half_width // HEAD
    gains_f = small_all[:, :4].astype(f32)
    router_f = small_all[:, 4:].astype(f32)
    gain_in = gains_f[:, 0]
    gain_mid = gains_f[:, 1]
    gain_q = lax.dynamic_slice_in_dim(gains_f[:, 2], tp_index * half_width, half_width)
    gain_k = lax.dynamic_slice_in_dim(gains_f[:, 3], tp_index * half_width, half_width)
    score_scale = HEAD ** (-0.5)
    seq_all, pos_all = places_info(token_order[0], lengths[0])

    def ctx_rows(table, index):
        return lax.dynamic_slice_in_dim(table, index * tokens, tokens)

    seq_mine, pos_mine = ctx_rows(seq_all, ctx_index), ctx_rows(pos_all, ctx_index)
    key_order = [ctx_index ^ step for step in range(ctx_size)]
    seq_keys = jnp.concatenate([ctx_rows(seq_all, i) for i in key_order])
    pos_keys = jnp.concatenate([ctx_rows(pos_all, i) for i in key_order])
    cosine, sine = rope_tables(pos_mine, HEAD)
    visible = (seq_mine[:, None] == seq_keys[None, :]) & (pos_keys[None, :] <= pos_mine[:, None])

    layer_f = layer_in.astype(f32)
    rate_in = lax.rsqrt(jnp.mean(layer_f * layer_f, axis=-1, keepdims=True) + norm_eps)
    in_hat = layer_f * rate_in
    in_low = (in_hat * gain_in).astype(bf16)
    qkv_mats = qkv_all.reshape(3, width, half_width)
    q_raw, k_raw, v_raw = (
        jnp.dot(in_low, qkv_mats[j], preferred_element_type=f32) for j in range(3)
    )
    v_low = v_raw.astype(bf16)
    square_q, square_k = lax.psum(
        (jnp.sum(q_raw * q_raw, axis=1), jnp.sum(k_raw * k_raw, axis=1)), "tp"
    )
    rate_q = lax.rsqrt(square_q / full_heads + norm_eps)[:, None]
    rate_k = lax.rsqrt(square_k / full_heads + norm_eps)[:, None]
    q_hat = q_raw * rate_q
    k_hat = k_raw * rate_k
    q_low = rotate((q_hat * gain_q).reshape(tokens, head_count, HEAD), cosine, sine).astype(bf16)
    k_low = (
        rotate((k_hat * gain_k).reshape(tokens, head_count, HEAD), cosine, sine)
        .astype(bf16)
        .reshape(tokens, half_width)
    )

    def gather_ctx(block):
        far = swap_ctx(block, 2)
        return jnp.concatenate([block, swap_ctx(block, 1), far, swap_ctx(far, 1)], axis=0)

    group_len = tokens * ctx_size
    with jax.named_scope("gather_values"):
        value_heads = gather_ctx(v_low).reshape(group_len, head_count, HEAD)
    with jax.named_scope("gather_keys"):
        key_heads = gather_ctx(k_low).reshape(group_len, head_count, HEAD)
    scores = jnp.einsum("qhd,khd->hqk", q_low, key_heads, preferred_element_type=f32) * score_scale
    scores = jnp.where(visible[None], scores, masked_score)
    row_max = jnp.max(scores, axis=-1, keepdims=True)
    shifted = jnp.exp(scores - row_max)
    row_sum = jnp.sum(shifted, axis=-1, keepdims=True)
    weights = shifted / row_sum
    log_total = row_max + jnp.log(row_sum)
    mixed = jnp.einsum(
        "hqk,khd->qhd", weights.astype(bf16), value_heads, preferred_element_type=f32
    )
    mixed_low = mixed.reshape(tokens, half_width).astype(bf16)
    attn_part = lax.dot_general(
        mixed_low, out_all, (((1,), (1,)), ((), ())), preferred_element_type=f32
    )
    attn = my_rows(attn_part) + swap_tp(other_rows(attn_part).astype(bf16)).astype(f32)

    resid = my_rows(layer_f) + attn
    rate_mid = lax.rsqrt(jnp.mean(resid * resid, axis=-1, keepdims=True) + norm_eps)
    mid_hat = resid * rate_mid
    mid_norm = mid_hat * gain_mid
    logits = jnp.dot(mid_norm, router_f, precision=highest)
    expert_ids = jnp.arange(experts, dtype=jnp.int32)
    chosen = jnp.any(my_rows(routes)[:, :, None] == expert_ids[None, None, :], axis=1)
    logits_max = jnp.max(jnp.where(chosen, logits, -jnp.inf), axis=-1, keepdims=True)
    gates = jnp.where(chosen, jnp.exp(jnp.where(chosen, logits - logits_max, 0.0)), 0.0)
    gates = gates / jnp.sum(gates, axis=-1, keepdims=True)

    def padded(parts):
        columns = sum(part.shape[1] for part in parts)
        rest = -columns % LANES
        if rest:
            parts = parts + [jnp.zeros((parts[0].shape[0], rest), parts[0].dtype)]
        return jnp.concatenate(parts, axis=1)

    shards = lax.axis_size("shard")
    shard_index = lax.axis_index("shard")
    steps = range(shards)

    def block_of(step, far, side):
        return ((shard_index + shards - step) % shards) * ctx_size + (
            ctx_index ^ (2 * far + side)
        )

    mid_block = padded([mid_norm.astype(bf16)] + split_three(gates))
    near_blocks = [mid_block] + [shift_shard(mid_block, step) for step in steps[1:]]
    far_blocks = [swap_ctx(block, 2) for block in near_blocks]
    near_group = jnp.concatenate(near_blocks, axis=0)
    far_group = jnp.concatenate(far_blocks, axis=0)
    mid_groups = [
        [near_group, swap_ctx(near_group, 1)],
        [far_group, swap_ctx(far_group, 1)],
    ]
    grad_groups = [
        [
            jnp.concatenate(
                [
                    lax.dynamic_slice_in_dim(grad_rows, block_of(step, far, side) * half, half)
                    for step in steps
                ],
                axis=0,
            )
            for side in range(2)
        ]
        for far in range(2)
    ]
    hidden_raws = [
        [jnp.dot(rows, w_back, preferred_element_type=f32) for rows in pair] for pair in grad_groups
    ]
    column = jnp.arange(mid_block.shape[1] - width, dtype=jnp.int32)
    mine_in = (column % experts == expert_index) & (column < 3 * experts)
    pads = -2 * experts % LANES + 2 * experts
    spot = jnp.arange(pads, dtype=jnp.int32)[None, :]
    zero = jnp.zeros((), bf16)

    def through_expert(rows, hidden_raw):
        extra = rows[:, width:].astype(f32)
        gate_col = jnp.sum(jnp.where(mine_in[None, :], extra, 0.0), axis=1, keepdims=True)
        both = jnp.dot(rows[:, :width], w_in, preferred_element_type=f32)
        gate_val, up_val = both[:, : 2 * hidden], both[:, 2 * hidden :]
        gate_sig = jax.nn.sigmoid(gate_val)
        gate_act = gate_val * gate_sig
        hidden_act = gate_act * up_val
        score_col = jnp.sum(hidden_act * hidden_raw, axis=1, keepdims=True)
        gated_act = (gate_col * hidden_act).astype(bf16)
        hidden_grad = gate_col * hidden_raw
        gate_grad = hidden_grad * up_val * gate_sig * (1.0 + gate_val * (1.0 - gate_sig))
        up_grad = hidden_grad * gate_act
        both_grad = jnp.concatenate([gate_grad.astype(bf16), up_grad.astype(bf16)], axis=1)
        mix_part = lax.dot_general(
            gated_act, w_back, (((1,), (1,)), ((), ())), preferred_element_type=f32
        ).astype(bf16)
        back_part = lax.dot_general(
            both_grad, w_in, (((1,), (1,)), ((), ())), preferred_element_type=f32
        ).astype(bf16)
        score_high = score_col.astype(bf16)
        score_rest = (score_col - score_high.astype(f32)).astype(bf16)
        score_part = jnp.where(
            spot == expert_index,
            score_high,
            jnp.where(spot == expert_index + experts, score_rest, zero),
        )
        return gated_act, both_grad, jnp.concatenate([mix_part, back_part, score_part], axis=1)

    through = [
        [through_expert(mid_groups[far][side], hidden_raws[far][side]) for side in range(2)]
        for far in range(2)
    ]

    def blocks_of(group):
        return [group[step * half : (step + 1) * half] for step in steps]

    def sum_side(far):
        arrived = swap_ctx(through[far][1][2], 1)
        return [
            add_low(mine, other).astype(bf16)
            for mine, other in zip(blocks_of(through[far][0][2]), blocks_of(arrived))
        ]

    far_sums, near_sums = sum_side(1), sum_side(0)
    block_sums = [
        add_low(mine, swap_ctx(other, 2)) for mine, other in zip(near_sums, far_sums)
    ]
    block_total = block_sums[0]
    for step in steps[1:]:
        block_total = block_total + shift_shard(block_sums[step].astype(bf16), -step).astype(f32)

    def all_rows(table):
        return jnp.concatenate([table[far][side] for far in range(2) for side in range(2)], axis=0)

    in_grad = lax.dot_general(
        all_rows(mid_groups)[:, :width],
        all_rows([[entry[1] for entry in pair] for pair in through]),
        (((0,), (0,)), ((), ())),
        preferred_element_type=f32,
    )
    back_grad = lax.dot_general(
        all_rows(grad_groups),
        all_rows([[entry[0] for entry in pair] for pair in through]),
        (((0,), (0,)), ((), ())),
        preferred_element_type=f32,
    )
    grads_other = jnp.concatenate(
        [
            hidden_part(in_grad, 1).astype(bf16),
            hidden_part(in_grad, 3).astype(bf16),
            hidden_part(back_grad, 1).astype(bf16),
        ],
        axis=1,
    )
    with jax.named_scope("swap_grads"):
        grads_arrived = swap_tp(grads_other)
    gate_up_grad = jnp.stack(
        [
            hidden_part(in_grad, 0) + hidden_part(grads_arrived, 0).astype(f32),
            hidden_part(in_grad, 2) + hidden_part(grads_arrived, 1).astype(f32),
        ],
        axis=1,
    )[None]
    down_grad = (hidden_part(back_grad, 0) + hidden_part(grads_arrived, 2).astype(f32))[None]

    mixture = block_total[:, :width]
    mid_grad = block_total[:, width : 2 * width]
    scores_in = block_total[:, 2 * width :]
    score_total = scores_in[:, :experts] + scores_in[:, experts : 2 * experts]
    output_half = (resid + mixture).astype(bf16)
    output = join_halves(output_half, swap_tp(output_half), first_is_mine)
    logit_grad = gates * (score_total - jnp.sum(gates * score_total, axis=1, keepdims=True))
    router_grad = lax.dot_general(
        logit_grad, mid_norm, (((0,), (0,)), ((), ())), precision=highest
    )
    mid_grad = mid_grad + lax.dot_general(
        logit_grad, router_f, (((1,), (1,)), ((), ())), precision=highest
    )
    mid_scaled = gain_mid * mid_grad
    resid_grad = grad_half.astype(f32) + rate_mid * (
        mid_scaled - mid_hat * jnp.mean(mid_hat * mid_scaled, axis=-1, keepdims=True)
    )
    gain_mid_grad = jnp.sum(mid_grad * mid_hat, axis=0, keepdims=True)
    attn_half = resid_grad.astype(bf16)
    attn_low = join_halves(attn_half, swap_tp(attn_half), first_is_mine)
    out_proj_grad = lax.dot_general(
        attn_low, mixed_low, (((0,), (0,)), ((), ())), preferred_element_type=f32
    ).astype(bf16)
    out_owned = lax.psum_scatter(
        out_proj_grad, owners, scatter_dimension=0, tiled=True
    ).astype(f32)
    mixed_grad = (
        jnp.dot(attn_low, out_all, preferred_element_type=f32)
        .astype(bf16)
        .reshape(tokens, head_count, HEAD)
    )
    again = jnp.einsum("qhd,khd->hqk", q_low, key_heads, preferred_element_type=f32) * score_scale
    again = jnp.where(visible[None], again, masked_score)
    weights_again = jnp.exp(again - log_total)
    weights_low = weights_again.astype(bf16)
    weight_grad = jnp.einsum("qhd,khd->hqk", mixed_grad, value_heads, preferred_element_type=f32)
    score_grad = weights_again * (
        weight_grad - jnp.sum(weights_again * weight_grad, axis=-1, keepdims=True)
    )
    score_low = score_grad.astype(bf16)
    q_grad = (
        jnp.einsum("hqk,khd->qhd", score_low, key_heads, preferred_element_type=f32) * score_scale
    )
    k_part = (
        jnp.einsum("hqk,qhd->khd", score_low, q_low, preferred_element_type=f32) * score_scale
    )
    v_part = jnp.einsum("hqk,qhd->khd", weights_low, mixed_grad, preferred_element_type=f32)

    kv_part = jnp.concatenate(
        [
            part.reshape(ctx_size, tokens, half_width).astype(bf16)
            for part in (k_part, v_part)
        ],
        axis=2,
    )
    kv_arrived = swap_ctx(jnp.stack([kv_part[1], kv_part[3]]), 1)
    kv_far = add_low(kv_part[2], kv_arrived[1]).astype(bf16)
    kv_grad = add_low(kv_part[0], kv_arrived[0], swap_ctx(kv_far, 2))
    k_grad, v_grad = kv_grad[:, :half_width], kv_grad[:, half_width:]
    q_in = rotate_back(q_grad, cosine, sine).reshape(tokens, half_width)
    k_in = rotate_back(k_grad.reshape(tokens, head_count, HEAD), cosine, sine).reshape(
        tokens, half_width
    )
    q_scaled = gain_q * q_in
    k_scaled = gain_k * k_in
    inner_q, inner_k = lax.psum(
        (jnp.sum(q_scaled * q_hat, axis=1), jnp.sum(k_scaled * k_hat, axis=1)), "tp"
    )
    q_raw_grad = rate_q * (q_scaled - q_hat * (inner_q / full_heads)[:, None])
    k_raw_grad = rate_k * (k_scaled - k_hat * (inner_k / full_heads)[:, None])
    raw_grads = [q_raw_grad.astype(bf16), k_raw_grad.astype(bf16), v_grad.astype(bf16)]
    raw_stack = jnp.stack(raw_grads)
    in_turned = in_low.T
    block_rows = w_qkv.shape[0]

    def grad_blocks(far, side, added=None):
        order = jnp.stack(
            [
                ((shard_index + step) % shards) * ctx_size + (ctx_index ^ (2 * far + side))
                for step in steps
            ]
        ).astype(jnp.int32)
        return weight_grad_blocks(order, in_turned, raw_stack, block_rows, added)

    far_grads = grad_blocks(1, 0, swap_ctx(grad_blocks(1, 1), 1))
    near_grads = grad_blocks(0, 0, swap_ctx(grad_blocks(0, 1), 1))
    step_grads = [add_low(near_grads[step], swap_ctx(far_grads[step], 2)) for step in steps]
    qkv_owned = step_grads[0]
    for step in steps[1:]:
        qkv_owned = qkv_owned + shift_shard(step_grads[step].astype(bf16), step).astype(f32)
    norm_part = sum(
        lax.dot_general(raw, mat, (((1,), (1,)), ((), ())), preferred_element_type=f32)
        for raw, mat in zip(raw_grads, (qkv_mats[0], qkv_mats[1], qkv_mats[2]))
    )
    in_norm_grad = my_rows(norm_part) + swap_tp(other_rows(norm_part).astype(bf16)).astype(f32)
    in_hat_half = my_rows(in_hat)
    in_scaled = gain_in * in_norm_grad
    input_half = resid_grad + my_rows(rate_in) * (
        in_scaled - in_hat_half * jnp.mean(in_hat_half * in_scaled, axis=-1, keepdims=True)
    )
    input_grad = join_halves(input_half, swap_tp(input_half), first_is_mine)
    gain_in_grad = jnp.sum(in_norm_grad * in_hat_half, axis=0, keepdims=True)
    gain_pair = jnp.stack([jnp.sum(q_in * q_hat, axis=0), jnp.sum(k_in * k_hat, axis=0)], axis=0)
    qk_gain_part = lax.dynamic_update_slice(
        jnp.zeros((2, width), f32), gain_pair, (0, tp_index * half_width)
    )
    early_total = sum_all(jnp.concatenate([router_grad, gain_mid_grad], axis=0))
    late_total = sum_all(jnp.concatenate([gain_in_grad, qk_gain_part], axis=0))
    gains_total = jnp.concatenate(
        [late_total[:1], early_total[experts:], late_total[1:]], axis=0
    )
    router_total = early_total[:experts]
    own_rows = norm_gains.shape[0]

    def owned(total):
        return lax.dynamic_slice_in_dim(total, expert_index * own_rows, own_rows, axis=1).T

    return (
        output,
        input_grad,
        qkv_owned,
        out_owned,
        owned(gains_total),
        owned(router_total),
        gate_up_grad,
        down_grad,
    )


def solution(mesh):
    in_specs = (
        P(("shard", "ctx"), None),
        P(("shard", "ctx"), "tp"),
        P(("shard", "ctx"), "tp"),
        P(("shard", "ctx"), None),
        P(("shard", "ctx"), None),
        P(("shard", "ctx"), None, None, "tp"),
        P(("shard", "ctx"), None, "tp"),
        P(("shard", "ctx"), None),
        P("shard", None),
        P("shard", None),
        P(("shard", "ctx"), None),
    )
    out_specs = (
        P(("shard", "ctx"), None),
        P(("shard", "ctx"), None),
        P(("shard", "ctx"), "tp"),
        P(("shard", "ctx"), "tp"),
        P(("shard", "ctx"), None),
        P(("shard", "ctx"), None),
        P(("shard", "ctx"), None, None, "tp"),
        P(("shard", "ctx"), None, "tp"),
    )
    return jax.shard_map(local, mesh=mesh, in_specs=in_specs, out_specs=out_specs, check_vma=False)
```

```python
import functools
import math

import jax
import jax.numpy as jnp
from jax import lax
from jax.experimental import pallas as pl
from jax.experimental.layout import Layout, with_layout_constraint
from jax.experimental.pallas import tpu as pltpu
from jax.sharding import PartitionSpec as P

HEAD = 128
LANES = 128


norm_eps = 1e-05
rope_base = 10000.0
masked_score = -1e30


def places_info(order_row, length_row):
    seq_ends = jnp.cumsum(length_row)
    seq_starts = seq_ends - length_row
    sequence = jnp.sum((order_row[:, None] >= seq_ends[None, :]).astype(jnp.int32), axis=1)
    picker = jnp.arange(length_row.shape[0], dtype=jnp.int32)[None, :] == sequence[:, None]
    first_place = jnp.sum(jnp.where(picker, seq_starts[None, :], 0), axis=1)
    return (sequence, order_row - first_place)


def rope_tables(place_pos, head_size):
    freq_index = jnp.arange(head_size // 2, dtype=jnp.float32)
    inverse = 1.0 / rope_base ** (freq_index * 2.0 / head_size)
    angle = place_pos.astype(jnp.float32)[:, None] * inverse[None, :]
    cosine = jnp.cos(angle)
    sine = jnp.sin(angle)
    return (jnp.concatenate([cosine, cosine], 1), jnp.concatenate([sine, sine], 1))


def rotate(values_in, cosine, sine):
    half_width = values_in.shape[-1] // 2
    turned = jnp.concatenate([-values_in[..., half_width:], values_in[..., :half_width]], -1)
    return values_in * cosine[:, None, :] + turned * sine[:, None, :]


def rotate_back(grad_in, cosine, sine):
    half_width = grad_in.shape[-1] // 2
    scaled = grad_in * sine[:, None, :]
    return grad_in * cosine[:, None, :] + jnp.concatenate(
        [scaled[..., half_width:], -scaled[..., :half_width]], -1
    )


def swap_tp(values_in):
    return lax.ppermute(values_in, "tp", [(0, 1), (1, 0)])


def swap_ctx(values_in, bit):
    return lax.ppermute(values_in, "ctx", [(i, i ^ bit) for i in range(lax.axis_size("ctx"))])


def shift_shard(values_in, step):
    size = lax.axis_size("shard")
    return lax.ppermute(values_in, "shard", [(i, (i + step) % size) for i in range(size)])


def row_major(values_in):
    return with_layout_constraint(values_in, Layout(major_to_minor=tuple(range(values_in.ndim))))


def add_low(first, *others):
    total = first.astype(jnp.float32)
    for other in others:
        total = total + other.astype(jnp.float32)
    return total


def weight_grad_kernel(sub, count, added, order_ref, rows_ref, raw_ref, *refs):
    step = pl.program_id(0)
    block = order_ref[step]
    outs = refs[1:] if added else refs
    pieces = outs[0].shape[-2] // sub
    totals = []
    for piece in range(pieces):
        granule = block * pieces + piece
        matrix = granule // count
        start = pl.multiple_of((granule % count) * sub, sub)
        total = jnp.dot(
            rows_ref[pl.ds(start, sub), :], raw_ref[matrix], preferred_element_type=jnp.float32
        )
        if added:
            total = total + refs[0][0, piece * sub : (piece + 1) * sub, :].astype(jnp.float32)
        totals.append(total.astype(jnp.bfloat16))
    whole = jnp.concatenate(totals, axis=0)
    if added:
        for position, out in enumerate(outs):

            @pl.when(step == position)
            def _(out=out):
                out[...] = whole
    else:
        outs[0][0] = whole


def weight_grad_blocks(order, rows, raw, block_rows, added=None):
    width, tokens = rows.shape
    columns = raw.shape[2]
    sub = math.gcd(block_rows, width)
    blocks = order.shape[0]
    block_spec = pl.BlockSpec((1, block_rows, columns), lambda i, order: (i, 0, 0))
    in_specs = [
        pl.BlockSpec((width, tokens), lambda i, order: (0, 0)),
        pl.BlockSpec(raw.shape, lambda i, order: (0, 0, 0)),
    ]
    operands = [rows, raw]
    if added is None:
        out_shape = jax.ShapeDtypeStruct((blocks, block_rows, columns), jnp.bfloat16)
        out_specs = block_spec
    else:
        in_specs.append(block_spec)
        operands.append(added)
        out_shape = [jax.ShapeDtypeStruct((block_rows, columns), jnp.bfloat16)] * blocks
        out_specs = [pl.BlockSpec((block_rows, columns), lambda i, order: (0, 0))] * blocks
    return pl.pallas_call(
        functools.partial(weight_grad_kernel, sub, width // sub, added is not None),
        out_shape=out_shape,
        grid_spec=pltpu.PrefetchScalarGridSpec(
            num_scalar_prefetch=1, grid=(blocks,), in_specs=in_specs, out_specs=out_specs
        ),
        cost_estimate=pl.CostEstimate(
            flops=2 * blocks * block_rows * tokens * columns,
            bytes_accessed=2 * blocks * block_rows * columns * len(in_specs),
            transcendentals=0,
        ),
    )(order, *operands)


def reorder_kernel(order_ref, rows_ref, out_ref):
    out_ref[...] = rows_ref[...]


def reorder_blocks(order, rows):
    spec = (1,) + rows.shape[1:]
    return pl.pallas_call(
        reorder_kernel,
        out_shape=jax.ShapeDtypeStruct(rows.shape, rows.dtype),
        grid_spec=pltpu.PrefetchScalarGridSpec(
            num_scalar_prefetch=1,
            grid=(rows.shape[0],),
            in_specs=[pl.BlockSpec(spec, lambda i, order: (order[i], 0, 0))],
            out_specs=pl.BlockSpec(spec, lambda i, order: (i, 0, 0)),
        ),
        cost_estimate=pl.CostEstimate(
            flops=0, bytes_accessed=2 * rows.size * rows.dtype.itemsize, transcendentals=0
        ),
    )(order, rows)


TILE = 256


def expert_in_kernel(experts, index_ref, rows_ref, grads_ref, *refs):
    f32, bf16 = jnp.float32, jnp.bfloat16
    weights, (act_ref, dgate_ref, dup_ref, score_ref) = refs[:6], refs[6:]
    width = weights[0].shape[0]
    tile = pl.program_id(0)

    def through(gate_ref, up_ref, back_ref):
        extra = rows_ref[:, width:].astype(f32)
        column = lax.broadcasted_iota(jnp.int32, extra.shape, 1)
        mine_in = (column % experts == index_ref[0]) & (column < 3 * experts)
        gate_col = jnp.sum(jnp.where(mine_in, extra, 0.0), axis=1, keepdims=True)
        rows = rows_ref[:, :width]
        gate_val = jnp.dot(rows, gate_ref[...], preferred_element_type=f32)
        up_val = jnp.dot(rows, up_ref[...], preferred_element_type=f32)
        hidden_raw = jnp.dot(grads_ref[0], back_ref[...], preferred_element_type=f32)
        gate_sig = jax.nn.sigmoid(gate_val)
        gate_act = gate_val * gate_sig
        hidden_act = gate_act * up_val
        act_ref[...] = (gate_col * hidden_act).astype(bf16)
        hidden_grad = gate_col * hidden_raw
        dgate = hidden_grad * up_val * gate_sig * (1.0 + gate_val * (1.0 - gate_sig))
        dgate_ref[...] = dgate.astype(bf16)
        dup_ref[...] = (hidden_grad * gate_act).astype(bf16)
        score = hidden_act * hidden_raw
        lanes = score[:, :LANES]
        for start in range(LANES, TILE, LANES):
            lanes = lanes + score[:, start : start + LANES]

        @pl.when(tile == 0)
        def _():
            score_ref[...] = lanes

        @pl.when(tile > 0)
        def _():
            score_ref[...] += lanes

    side = pl.num_programs(0) // 2

    @pl.when(tile < side)
    def _():
        through(*weights[:3])

    @pl.when(tile >= side)
    def _():
        through(*weights[3:])


def expert_in(index, rows, grads, group, own, other, experts):
    count, columns = rows.shape
    width, hidden = own[1].shape
    side = hidden // TILE

    def tiles(shift, base):
        return pl.BlockSpec(
            (width, TILE), lambda h, index: (0, base + jnp.clip(h - shift, 0, side - 1))
        )

    weight_specs = [tiles(shift, base) for shift in (0, side) for base in (0, side, 0)]
    wide = pl.BlockSpec((count, TILE), lambda h, index: (0, h))
    return pl.pallas_call(
        functools.partial(expert_in_kernel, experts),
        out_shape=[jax.ShapeDtypeStruct((count, 2 * hidden), jnp.bfloat16)] * 3
        + [jax.ShapeDtypeStruct((count, LANES), jnp.float32)],
        grid_spec=pltpu.PrefetchScalarGridSpec(
            num_scalar_prefetch=1,
            grid=(2 * side,),
            in_specs=[
                pl.BlockSpec((count, columns), lambda h, index: (0, 0)),
                pl.BlockSpec((1, count, width), lambda h, index: (group, 0, 0)),
            ]
            + weight_specs,
            out_specs=[wide, wide, wide, pl.BlockSpec((count, LANES), lambda h, index: (0, 0))],
        ),
        cost_estimate=pl.CostEstimate(
            flops=12 * count * width * hidden,
            bytes_accessed=12 * width * hidden,
            transcendentals=2 * count * hidden,
        ),
    )(index, rows, grads, own[0], own[0], own[1], other[0], other[0], other[1])


def expert_out_kernel(experts, added, index_ref, act_ref, dgate_ref, dup_ref, score_ref, *refs):
    f32, bf16 = jnp.float32, jnp.bfloat16
    down_own, pair_own, down_other, pair_other = refs[:4]
    outs = refs[5:] if added else refs[4:]
    hidden = down_own.shape[1]
    half = outs[0].shape[0]
    step = pl.program_id(0)
    side = pl.num_programs(0) // 2

    def times(rows, weights):
        return lax.dot_general(
            rows, weights, (((1,), (1,)), ((), ())), preferred_element_type=f32
        )

    def put(total):
        if added:
            total = total + refs[4][...].astype(f32)
        total = total.astype(bf16)
        for piece, out in enumerate(outs):
            out[...] = total[piece * half : (piece + 1) * half, :]

    @pl.when(step < side)
    def _():
        put(
            times(act_ref[:, :hidden], down_own[...])
            + times(act_ref[:, hidden:], down_other[...])
        )

    @pl.when((step >= side) & (step < 2 * side))
    def _():
        put(
            times(dgate_ref[:, :hidden], pair_own[:, :hidden])
            + times(dup_ref[:, :hidden], pair_own[:, hidden:])
            + times(dgate_ref[:, hidden:], pair_other[:, :hidden])
            + times(dup_ref[:, hidden:], pair_other[:, hidden:])
        )

    @pl.when(step == 2 * side)
    def _():
        score = jnp.sum(score_ref[...], axis=1, keepdims=True)
        high = score.astype(bf16).astype(f32)
        spot = lax.broadcasted_iota(jnp.int32, (score.shape[0], TILE), 1)
        rest = jnp.where(spot == index_ref[0] + experts, score - high, 0.0)
        put(jnp.where(spot == index_ref[0], high, rest))


def expert_out(index, act, dgate, dup, score, own, other, experts, pieces, added=None):
    count = act.shape[0]
    width, hidden = own[1].shape
    side = width // TILE
    total = (2 * side + 1) * TILE
    whole = pl.BlockSpec((count, 2 * hidden), lambda n, index: (0, 0))
    wide = pl.BlockSpec((count, TILE), lambda n, index: (0, n))
    down_spec = pl.BlockSpec((TILE, hidden), lambda n, index: (jnp.minimum(n, side - 1), 0))
    pair_spec = pl.BlockSpec(
        (TILE, 2 * hidden), lambda n, index: (jnp.clip(n - side, 0, side - 1), 0)
    )
    in_specs = [
        whole,
        whole,
        whole,
        pl.BlockSpec((count, LANES), lambda n, index: (0, 0)),
        down_spec,
        pair_spec,
        down_spec,
        pair_spec,
    ]
    operands = [act, dgate, dup, score, own[1], own[0], other[1], other[0]]
    if added is not None:
        in_specs.append(wide)
        operands.append(added)
    rows = count // pieces
    return pl.pallas_call(
        functools.partial(expert_out_kernel, experts, added is not None),
        out_shape=[jax.ShapeDtypeStruct((rows, total), jnp.bfloat16)] * pieces,
        grid_spec=pltpu.PrefetchScalarGridSpec(
            num_scalar_prefetch=1,
            grid=(2 * side + 1,),
            in_specs=in_specs,
            out_specs=[pl.BlockSpec((rows, TILE), lambda n, index: (0, n))] * pieces,
        ),
        cost_estimate=pl.CostEstimate(
            flops=12 * count * width * hidden,
            bytes_accessed=12 * width * hidden + 4 * count * total,
            transcendentals=0,
        ),
    )(index, *operands)


def join_halves(mine, other, first_is_mine):
    top = jnp.where(first_is_mine, mine, other)
    bottom = jnp.where(first_is_mine, other, mine)
    return jnp.concatenate([top, bottom], axis=0)


def split_three(values_in):
    high = values_in.astype(jnp.bfloat16)
    rest = values_in - high.astype(jnp.float32)
    middle = rest.astype(jnp.bfloat16)
    low = (rest - middle.astype(jnp.float32)).astype(jnp.bfloat16)
    return [high, middle, low]


def local(
    layer_in,
    w_qkv,
    w_out,
    norm_gains,
    router,
    w_gate_up,
    w_down,
    routes,
    lengths,
    token_order,
    out_grad,
):
    bf16, f32 = jnp.bfloat16, jnp.float32
    highest = lax.Precision.HIGHEST
    tokens, width = layer_in.shape
    experts = router.shape[1]
    hidden = w_down.shape[2]
    half = tokens // 2
    owners = ("shard", "ctx")
    tp_index = lax.axis_index("tp")
    ctx_index = lax.axis_index("ctx")
    ctx_size = lax.axis_size("ctx")
    expert_index = lax.axis_index("shard") * ctx_size + ctx_index
    first_is_mine = tp_index == 0
    my_row = tp_index * half
    other_row = (1 - tp_index) * half

    def my_rows(values_in):
        return lax.dynamic_slice_in_dim(values_in, my_row, half)

    def other_rows(values_in):
        return lax.dynamic_slice_in_dim(values_in, other_row, half)

    small_all = lax.all_gather(
        jnp.concatenate([norm_gains, router], axis=1), owners, axis=0, tiled=True
    )
    qkv_all = lax.all_gather(w_qkv, owners, axis=0, tiled=True)
    out_all = lax.all_gather(w_out, owners, axis=0, tiled=True)
    grad_half = my_rows(out_grad)
    grad_rows = lax.all_gather(grad_half, owners, axis=0, tiled=True)
    pair_own = jnp.concatenate([w_gate_up[0, :, 0], w_gate_up[0, :, 1]], axis=1)
    pair_other = swap_tp(pair_own)

    def hidden_part(which, index):
        return which[:, index * hidden : (index + 1) * hidden]

    half_width = qkv_all.shape[1]
    full_heads = half_width * lax.axis_size("tp")
    head_count = half_width // HEAD
    gains_f = small_all[:, :4].astype(f32)
    router_f = small_all[:, 4:].astype(f32)
    gain_in = gains_f[:, 0]
    gain_mid = gains_f[:, 1]
    gain_q = lax.dynamic_slice_in_dim(gains_f[:, 2], tp_index * half_width, half_width)
    gain_k = lax.dynamic_slice_in_dim(gains_f[:, 3], tp_index * half_width, half_width)
    score_scale = HEAD ** (-0.5)
    seq_all, pos_all = places_info(token_order[0], lengths[0])

    def ctx_rows(table, index):
        return lax.dynamic_slice_in_dim(table, index * tokens, tokens)

    seq_mine, pos_mine = ctx_rows(seq_all, ctx_index), ctx_rows(pos_all, ctx_index)
    key_order = [ctx_index ^ step for step in range(ctx_size)]
    seq_keys = jnp.concatenate([ctx_rows(seq_all, i) for i in key_order])
    pos_keys = jnp.concatenate([ctx_rows(pos_all, i) for i in key_order])
    cosine, sine = rope_tables(pos_mine, HEAD)
    visible = (seq_mine[:, None] == seq_keys[None, :]) & (pos_keys[None, :] <= pos_mine[:, None])

    layer_f = layer_in.astype(f32)
    rate_in = lax.rsqrt(jnp.mean(layer_f * layer_f, axis=-1, keepdims=True) + norm_eps)
    in_hat = layer_f * rate_in
    in_low = row_major((in_hat * gain_in).astype(bf16))
    qkv_mats = qkv_all.reshape(3, width, half_width)
    q_raw, k_raw, v_raw = (
        jnp.dot(in_low, qkv_mats[j], preferred_element_type=f32) for j in range(3)
    )
    v_low = v_raw.astype(bf16)
    square_q, square_k = lax.psum(
        (jnp.sum(q_raw * q_raw, axis=1), jnp.sum(k_raw * k_raw, axis=1)), "tp"
    )
    down_own = lax.optimization_barrier((w_down[0], square_q))[0]
    down_other = swap_tp(down_own)
    own_weights, other_weights = (pair_own, w_down[0]), (pair_other, down_other)
    rate_q = lax.rsqrt(square_q / full_heads + norm_eps)[:, None]
    rate_k = lax.rsqrt(square_k / full_heads + norm_eps)[:, None]
    q_hat = q_raw * rate_q
    k_hat = k_raw * rate_k
    q_low = rotate((q_hat * gain_q).reshape(tokens, head_count, HEAD), cosine, sine).astype(bf16)
    k_low = (
        rotate((k_hat * gain_k).reshape(tokens, head_count, HEAD), cosine, sine)
        .astype(bf16)
        .reshape(tokens, half_width)
    )

    def gather_ctx(block):
        far = swap_ctx(block, 2)
        return jnp.concatenate([block, swap_ctx(block, 1), far, swap_ctx(far, 1)], axis=0)

    group_len = tokens * ctx_size
    value_heads = gather_ctx(v_low).reshape(group_len, head_count, HEAD)
    key_heads = gather_ctx(k_low).reshape(group_len, head_count, HEAD)
    scores = jnp.einsum("qhd,khd->hqk", q_low, key_heads, preferred_element_type=f32) * score_scale
    scores = jnp.where(visible[None], scores, masked_score)
    row_max = jnp.max(scores, axis=-1, keepdims=True)
    shifted = jnp.exp(scores - row_max)
    row_sum = jnp.sum(shifted, axis=-1, keepdims=True)
    weights = shifted / row_sum
    log_total = row_max + jnp.log(row_sum)
    mixed = jnp.einsum(
        "hqk,khd->qhd", weights.astype(bf16), value_heads, preferred_element_type=f32
    )
    mixed_low = mixed.reshape(tokens, half_width).astype(bf16)
    attn_part = lax.dot_general(
        mixed_low, out_all, (((1,), (1,)), ((), ())), preferred_element_type=f32
    )
    attn_part = row_major(attn_part)
    attn = my_rows(attn_part) + swap_tp(other_rows(attn_part).astype(bf16)).astype(f32)

    resid = my_rows(layer_f) + attn
    rate_mid = lax.rsqrt(jnp.mean(resid * resid, axis=-1, keepdims=True) + norm_eps)
    mid_hat = resid * rate_mid
    mid_norm = mid_hat * gain_mid
    logits = jnp.dot(mid_norm, router_f, precision=highest)
    expert_ids = jnp.arange(experts, dtype=jnp.int32)
    chosen = jnp.any(my_rows(routes)[:, :, None] == expert_ids[None, None, :], axis=1)
    logits_max = jnp.max(jnp.where(chosen, logits, -jnp.inf), axis=-1, keepdims=True)
    gates = jnp.where(chosen, jnp.exp(jnp.where(chosen, logits - logits_max, 0.0)), 0.0)
    gates = gates / jnp.sum(gates, axis=-1, keepdims=True)

    def padded(parts):
        columns = sum(part.shape[1] for part in parts)
        rest = -columns % LANES
        if rest:
            parts = parts + [jnp.zeros((parts[0].shape[0], rest), parts[0].dtype)]
        return jnp.concatenate(parts, axis=1)

    shards = lax.axis_size("shard")
    shard_index = lax.axis_index("shard")
    steps = range(shards)

    def block_of(step, far, side):
        return ((shard_index + shards - step) % shards) * ctx_size + (
            ctx_index ^ (2 * far + side)
        )

    mid_block = row_major(padded([mid_norm.astype(bf16)] + split_three(gates)))
    near_blocks = [mid_block] + [shift_shard(mid_block, step) for step in steps[1:]]
    far_blocks = [swap_ctx(block, 2) for block in near_blocks]
    near_group = row_major(jnp.concatenate(near_blocks, axis=0))
    far_group = row_major(jnp.concatenate(far_blocks, axis=0))
    mid_groups = [
        [near_group, swap_ctx(near_group, 1)],
        [far_group, swap_ctx(far_group, 1)],
    ]
    turn_order = jnp.stack(
        [block_of(step, far, side) for far in range(2) for side in range(2) for step in steps]
    ).astype(jnp.int32)
    grad_groups = reorder_blocks(turn_order, grad_rows.reshape(-1, half, width)).reshape(
        4, shards * half, width
    )
    index = expert_index.astype(jnp.int32).reshape(1)
    inside = {
        (far, side): expert_in(
            index, mid_groups[far][side], grad_groups, 2 * far + side, own_weights, other_weights, experts
        )
        for far in range(2)
        for side in range(2)
    }

    def sum_side(far):
        sent = expert_out(index, *inside[far, 1], own_weights, other_weights, experts, 1)[0]
        return expert_out(
            index,
            *inside[far, 0],
            own_weights,
            other_weights,
            experts,
            shards,
            swap_ctx(sent, 1),
        )

    far_sums = sum_side(1)
    far_arrived = [swap_ctx(far_sums[step], 2) for step in steps]
    near_sums = sum_side(0)
    block_sums = [add_low(mine, other) for mine, other in zip(near_sums, far_arrived)]
    step_arrived = [
        shift_shard(block_sums[step].astype(bf16), -step) for step in steps[1:]
    ]
    block_total = row_major(add_low(block_sums[0], *step_arrived))

    pairs = [(far, side) for far in range(2) for side in range(2)]
    mid_all = jnp.concatenate([mid_groups[far][side][:, :width] for far, side in pairs], axis=0)
    act_all, dgate_all, dup_all = (
        jnp.concatenate([inside[pair][which] for pair in pairs], axis=0) for which in range(3)
    )
    grad_all = grad_groups.reshape(-1, width)

    def over_tokens(rows, columns):
        return lax.dot_general(
            rows, columns, (((0,), (0,)), ((), ())), preferred_element_type=f32
        )

    pair_rows = jnp.concatenate(
        [hidden_part(dgate_all, 1), hidden_part(dup_all, 1)], axis=1
    )
    pair_sent = over_tokens(mid_all, pair_rows).astype(bf16)
    pair_arrived = swap_tp(pair_sent)
    gate_up_grad = jnp.stack(
        [
            over_tokens(mid_all, hidden_part(which, 0))
            + hidden_part(pair_arrived, position).astype(f32)
            for position, which in enumerate((dgate_all, dup_all))
        ],
        axis=1,
    )[None]
    down_sent = over_tokens(grad_all, hidden_part(act_all, 1)).astype(bf16)

    mixture = block_total[:, :width]
    mid_grad = block_total[:, width : 2 * width]
    scores_in = block_total[:, 2 * width :]
    score_total = scores_in[:, :experts] + scores_in[:, experts : 2 * experts]
    output_half = (resid + mixture).astype(bf16)
    output = join_halves(output_half, swap_tp(output_half), first_is_mine)
    logit_grad = gates * (score_total - jnp.sum(gates * score_total, axis=1, keepdims=True))
    router_grad = lax.dot_general(
        logit_grad, mid_norm, (((0,), (0,)), ((), ())), precision=highest
    )
    mid_grad = mid_grad + lax.dot_general(
        logit_grad, router_f, (((1,), (1,)), ((), ())), precision=highest
    )
    mid_scaled = gain_mid * mid_grad
    resid_grad = grad_half.astype(f32) + rate_mid * (
        mid_scaled - mid_hat * jnp.mean(mid_hat * mid_scaled, axis=-1, keepdims=True)
    )
    gain_mid_grad = jnp.sum(mid_grad * mid_hat, axis=0, keepdims=True)
    attn_half = resid_grad.astype(bf16)
    attn_low = join_halves(attn_half, swap_tp(attn_half), first_is_mine)
    out_proj_grad = lax.dot_general(
        attn_low, mixed_low, (((0,), (0,)), ((), ())), preferred_element_type=f32
    ).astype(bf16)
    out_owned = lax.psum_scatter(out_proj_grad, owners, scatter_dimension=0, tiled=True)
    out_owned = out_owned.astype(f32)
    mixed_grad = (
        jnp.dot(attn_low, out_all, preferred_element_type=f32)
        .astype(bf16)
        .reshape(tokens, head_count, HEAD)
    )
    again = jnp.einsum("qhd,khd->hqk", q_low, key_heads, preferred_element_type=f32) * score_scale
    again = jnp.where(visible[None], again, masked_score)
    weights_again = jnp.exp(again - log_total)
    weights_low = weights_again.astype(bf16)
    weight_grad = jnp.einsum("qhd,khd->hqk", mixed_grad, value_heads, preferred_element_type=f32)
    score_grad = weights_again * (
        weight_grad - jnp.sum(weights_again * weight_grad, axis=-1, keepdims=True)
    )
    score_low = score_grad.astype(bf16)
    q_grad = (
        jnp.einsum("hqk,khd->qhd", score_low, key_heads, preferred_element_type=f32) * score_scale
    )
    k_part = (
        jnp.einsum("hqk,qhd->khd", score_low, q_low, preferred_element_type=f32) * score_scale
    )
    v_part = jnp.einsum("hqk,qhd->khd", weights_low, mixed_grad, preferred_element_type=f32)

    kv_part = jnp.concatenate(
        [
            part.reshape(ctx_size, tokens, half_width).astype(bf16)
            for part in (k_part, v_part)
        ],
        axis=2,
    )
    kv_arrived = swap_ctx(jnp.stack([kv_part[1], kv_part[3]]), 1)
    kv_far = add_low(kv_part[2], kv_arrived[1]).astype(bf16)
    kv_grad = add_low(kv_part[0], kv_arrived[0], swap_ctx(kv_far, 2))
    k_grad, v_grad = kv_grad[:, :half_width], kv_grad[:, half_width:]
    q_in = rotate_back(q_grad, cosine, sine).reshape(tokens, half_width)
    k_in = rotate_back(k_grad.reshape(tokens, head_count, HEAD), cosine, sine).reshape(
        tokens, half_width
    )
    q_scaled = gain_q * q_in
    k_scaled = gain_k * k_in
    inner_q, inner_k = lax.psum(
        (jnp.sum(q_scaled * q_hat, axis=1), jnp.sum(k_scaled * k_hat, axis=1)), "tp"
    )
    down_sent = lax.optimization_barrier((down_sent, inner_q))[0]
    down_arrived = swap_tp(down_sent)
    down_grad = (over_tokens(grad_all, hidden_part(act_all, 0)) + down_arrived.astype(f32))[None]
    q_raw_grad = rate_q * (q_scaled - q_hat * (inner_q / full_heads)[:, None])
    k_raw_grad = rate_k * (k_scaled - k_hat * (inner_k / full_heads)[:, None])
    raw_grads = [q_raw_grad.astype(bf16), k_raw_grad.astype(bf16), v_grad.astype(bf16)]
    raw_stack = jnp.stack(raw_grads)
    in_turned = in_low.T
    block_rows = w_qkv.shape[0]

    def grad_blocks(far, side, added=None):
        order = jnp.stack(
            [
                ((shard_index + step) % shards) * ctx_size + (ctx_index ^ (2 * far + side))
                for step in steps
            ]
        ).astype(jnp.int32)
        return weight_grad_blocks(order, in_turned, raw_stack, block_rows, added)

    far_grads = grad_blocks(1, 0, swap_ctx(grad_blocks(1, 1), 1))
    far_grads_in = [swap_ctx(far_grads[step], 2) for step in steps]
    near_grads = grad_blocks(0, 0, swap_ctx(grad_blocks(0, 1), 1))
    step_grads = [add_low(near_grads[step], far_grads_in[step]) for step in steps]
    step_grads_in = [shift_shard(step_grads[step].astype(bf16), step) for step in steps[1:]]
    qkv_owned = add_low(step_grads[0], *step_grads_in)
    norm_part = sum(
        lax.dot_general(raw, mat, (((1,), (1,)), ((), ())), preferred_element_type=f32)
        for raw, mat in zip(raw_grads, (qkv_mats[0], qkv_mats[1], qkv_mats[2]))
    )
    norm_arrived = swap_tp(other_rows(norm_part).astype(bf16))
    in_norm_grad = my_rows(norm_part) + norm_arrived.astype(f32)
    in_hat_half = my_rows(in_hat)
    in_scaled = gain_in * in_norm_grad
    input_half = resid_grad + my_rows(rate_in) * (
        in_scaled - in_hat_half * jnp.mean(in_hat_half * in_scaled, axis=-1, keepdims=True)
    )
    input_grad = join_halves(input_half, swap_tp(input_half), first_is_mine)
    gain_in_grad = jnp.sum(in_norm_grad * in_hat_half, axis=0, keepdims=True)
    gain_pair = jnp.stack([jnp.sum(q_in * q_hat, axis=0), jnp.sum(k_in * k_hat, axis=0)], axis=0)
    qk_gain_part = lax.dynamic_update_slice(
        jnp.zeros((2, width), f32), gain_pair, (0, tp_index * half_width)
    )
    everyone = ("shard", "ctx", "tp")
    small_total = lax.psum(
        jnp.concatenate([gain_in_grad, gain_mid_grad, qk_gain_part, router_grad], axis=0),
        everyone,
    )
    small_owned = lax.dynamic_slice_in_dim(
        small_total, expert_index * norm_gains.shape[0], norm_gains.shape[0], axis=1
    ).T
    return (
        output,
        input_grad,
        qkv_owned,
        out_owned,
        small_owned[:, :4],
        small_owned[:, 4:],
        gate_up_grad,
        down_grad,
    )


def solution(mesh):
    in_specs = (
        P(("shard", "ctx"), None),
        P(("shard", "ctx"), "tp"),
        P(("shard", "ctx"), "tp"),
        P(("shard", "ctx"), None),
        P(("shard", "ctx"), None),
        P(("shard", "ctx"), None, None, "tp"),
        P(("shard", "ctx"), None, "tp"),
        P(("shard", "ctx"), None),
        P("shard", None),
        P("shard", None),
        P(("shard", "ctx"), None),
    )
    out_specs = (
        P(("shard", "ctx"), None),
        P(("shard", "ctx"), None),
        P(("shard", "ctx"), "tp"),
        P(("shard", "ctx"), "tp"),
        P(("shard", "ctx"), None),
        P(("shard", "ctx"), None),
        P(("shard", "ctx"), None, None, "tp"),
        P(("shard", "ctx"), None, "tp"),
    )

    return jax.shard_map(local, mesh=mesh, in_specs=in_specs, out_specs=out_specs, check_vma=False)
```

```python
import functools
import math

import jax
import jax.numpy as jnp
from jax import lax
from jax.experimental import pallas as pl
from jax.experimental.layout import Layout, with_layout_constraint
from jax.experimental.pallas import tpu as pltpu
from jax.sharding import PartitionSpec as P

HEAD = 128
LANES = 128
SHARD, CTX, TP = "shard", "ctx", "tp"
OWNERS = (SHARD, CTX)


norm_eps = 1e-05
rope_base = 10000.0
masked_score = -1e30


def places_info(order_row, length_row):
    seq_ends = jnp.cumsum(length_row)
    seq_starts = seq_ends - length_row
    sequence = jnp.sum((order_row[:, None] >= seq_ends[None, :]).astype(jnp.int32), axis=1)
    picker = jnp.arange(length_row.shape[0], dtype=jnp.int32)[None, :] == sequence[:, None]
    first_place = jnp.sum(jnp.where(picker, seq_starts[None, :], 0), axis=1)
    return (sequence, order_row - first_place)


def rope_tables(place_pos, head_size):
    freq_index = jnp.arange(head_size // 2, dtype=jnp.float32)
    inverse = 1.0 / rope_base ** (freq_index * 2.0 / head_size)
    angle = place_pos.astype(jnp.float32)[:, None] * inverse[None, :]
    cosine = jnp.cos(angle)
    sine = jnp.sin(angle)
    return (jnp.concatenate([cosine, cosine], 1), jnp.concatenate([sine, sine], 1))


def rotate(values_in, cosine, sine):
    half_width = values_in.shape[-1] // 2
    turned = jnp.concatenate([-values_in[..., half_width:], values_in[..., :half_width]], -1)
    return values_in * cosine[:, None, :] + turned * sine[:, None, :]


def rotate_back(grad_in, cosine, sine):
    half_width = grad_in.shape[-1] // 2
    scaled = grad_in * sine[:, None, :]
    return grad_in * cosine[:, None, :] + jnp.concatenate(
        [scaled[..., half_width:], -scaled[..., :half_width]], -1
    )


def swap_tp(values_in):
    return lax.ppermute(values_in, TP, [(0, 1), (1, 0)])


def swap_ctx(values_in, bit):
    return lax.ppermute(values_in, CTX, [(i, i ^ bit) for i in range(lax.axis_size(CTX))])


def shift_shard(values_in, step):
    size = lax.axis_size(SHARD)
    return lax.ppermute(values_in, SHARD, [(i, (i + step) % size) for i in range(size)])


def row_major(values_in):
    return with_layout_constraint(values_in, Layout(major_to_minor=tuple(range(values_in.ndim))))


def add_low(first, *others):
    total = first.astype(jnp.float32)
    for other in others:
        total = total + other.astype(jnp.float32)
    return total


def weight_grad_kernel(sub, count, added, order_ref, rows_ref, raw_ref, *refs):
    step = pl.program_id(0)
    block = order_ref[step]
    outs = refs[1:] if added else refs
    pieces = outs[0].shape[-2] // sub
    totals = []
    for piece in range(pieces):
        granule = block * pieces + piece
        matrix = granule // count
        start = pl.multiple_of((granule % count) * sub, sub)
        total = jnp.dot(
            rows_ref[pl.ds(start, sub), :], raw_ref[matrix], preferred_element_type=jnp.float32
        )
        if added:
            total = total + refs[0][0, piece * sub : (piece + 1) * sub, :].astype(jnp.float32)
        totals.append(total.astype(jnp.bfloat16))
    whole = jnp.concatenate(totals, axis=0)
    if added:
        for position, out in enumerate(outs):

            @pl.when(step == position)
            def _(out=out):
                out[...] = whole
    else:
        outs[0][0] = whole


def weight_grad_blocks(order, rows, raw, block_rows, added=None):
    width, tokens = rows.shape
    columns = raw.shape[2]
    sub = math.gcd(block_rows, width)
    blocks = order.shape[0]
    block_spec = pl.BlockSpec((1, block_rows, columns), lambda i, order: (i, 0, 0))
    in_specs = [
        pl.BlockSpec((width, tokens), lambda i, order: (0, 0)),
        pl.BlockSpec(raw.shape, lambda i, order: (0, 0, 0)),
    ]
    operands = [rows, raw]
    if added is None:
        out_shape = jax.ShapeDtypeStruct((blocks, block_rows, columns), jnp.bfloat16)
        out_specs = block_spec
    else:
        in_specs.append(block_spec)
        operands.append(added)
        out_shape = [jax.ShapeDtypeStruct((block_rows, columns), jnp.bfloat16)] * blocks
        out_specs = [pl.BlockSpec((block_rows, columns), lambda i, order: (0, 0))] * blocks
    return pl.pallas_call(
        functools.partial(weight_grad_kernel, sub, width // sub, added is not None),
        out_shape=out_shape,
        grid_spec=pltpu.PrefetchScalarGridSpec(
            num_scalar_prefetch=1, grid=(blocks,), in_specs=in_specs, out_specs=out_specs
        ),
        cost_estimate=pl.CostEstimate(
            flops=2 * blocks * block_rows * tokens * columns,
            bytes_accessed=2 * blocks * block_rows * columns * len(in_specs),
            transcendentals=0,
        ),
    )(order, *operands)


TILE = 256


def expert_in_kernel(experts, index_ref, *refs):
    f32, bf16 = jnp.float32, jnp.bfloat16
    rows_refs, grads_refs, weights = refs[:2], refs[2:4], refs[4:10]
    act_ref, dgate_ref, dup_ref, score_ref = refs[10:]
    width, count = weights[0].shape[0], rows_refs[0].shape[0]
    tile = pl.program_id(0)

    def through(gate_ref, up_ref, back_ref):
        for side in range(2):
            here = slice(side * count, (side + 1) * count)
            extra = rows_refs[side][:, width:].astype(f32)
            column = lax.broadcasted_iota(jnp.int32, extra.shape, 1)
            mine_in = (column % experts == index_ref[0]) & (column < 3 * experts)
            gate_col = jnp.sum(jnp.where(mine_in, extra, 0.0), axis=1, keepdims=True)
            rows = rows_refs[side][:, :width]
            gate_val = jnp.dot(rows, gate_ref[...], preferred_element_type=f32)
            up_val = jnp.dot(rows, up_ref[...], preferred_element_type=f32)
            hidden_raw = jnp.dot(grads_refs[side][...], back_ref[...], preferred_element_type=f32)
            gate_sig = jax.nn.sigmoid(gate_val)
            gate_act = gate_val * gate_sig
            hidden_act = gate_act * up_val
            act_ref[here, :] = (gate_col * hidden_act).astype(bf16)
            hidden_grad = gate_col * hidden_raw
            dgate = hidden_grad * up_val * gate_sig * (1.0 + gate_val * (1.0 - gate_sig))
            dgate_ref[here, :] = dgate.astype(bf16)
            dup_ref[here, :] = (hidden_grad * gate_act).astype(bf16)
            score = hidden_act * hidden_raw
            lanes = score[:, :LANES]
            for start in range(LANES, TILE, LANES):
                lanes = lanes + score[:, start : start + LANES]
            before = jnp.where(tile == 0, 0.0, score_ref[here, :])
            score_ref[here, :] = before + lanes

    side_tiles = pl.num_programs(0) // 2

    @pl.when(tile < side_tiles)
    def _():
        through(*weights[:3])

    @pl.when(tile >= side_tiles)
    def _():
        through(*weights[3:])


def expert_in(index, rows, grads, own, other, experts):
    count, columns = rows[0].shape
    width, hidden = own[1].shape
    side = hidden // TILE

    def tiles(shift, base):
        return pl.BlockSpec(
            (width, TILE), lambda h, index: (0, base + jnp.clip(h - shift, 0, side - 1))
        )

    weight_specs = [tiles(shift, base) for shift in (0, side) for base in (0, side, 0)]
    wide = pl.BlockSpec((2 * count, TILE), lambda h, index: (0, h))
    return pl.pallas_call(
        functools.partial(expert_in_kernel, experts),
        out_shape=[jax.ShapeDtypeStruct((2 * count, 2 * hidden), jnp.bfloat16)] * 3
        + [jax.ShapeDtypeStruct((2 * count, LANES), jnp.float32)],
        grid_spec=pltpu.PrefetchScalarGridSpec(
            num_scalar_prefetch=1,
            grid=(2 * side,),
            in_specs=[fixed((count, columns))] * 2 + [fixed((count, width))] * 2 + weight_specs,
            out_specs=[wide, wide, wide, fixed((2 * count, LANES))],
        ),
        cost_estimate=pl.CostEstimate(
            flops=24 * count * width * hidden,
            bytes_accessed=12 * width * hidden,
            transcendentals=4 * count * hidden,
        ),
    )(index, *rows, *grads, own[0], own[0], own[1], other[0], other[0], other[1])


def fixed(shape):
    return pl.BlockSpec(
        shape, lambda h, index: (0,) * len(shape), pipeline_mode=pl.Buffered(1)
    )


def expert_out_kernel(added, act_ref, dgate_ref, dup_ref, *refs):
    f32, bf16 = jnp.float32, jnp.bfloat16
    down_own, pair_own, down_other, pair_other = refs[:4]
    outs = refs[5:] if added else refs[4:]
    hidden = down_own.shape[1]
    half = outs[0].shape[0]
    step = pl.program_id(0)
    side = pl.num_programs(0) // 2

    def times(rows, weights):
        return lax.dot_general(
            rows, weights, (((1,), (1,)), ((), ())), preferred_element_type=f32
        )

    def put(total):
        if added:
            total = total + refs[4][...].astype(f32)
        total = total.astype(bf16)
        for piece, out in enumerate(outs):
            out[...] = total[piece * half : (piece + 1) * half, :]

    @pl.when(step < side)
    def _():
        put(
            times(act_ref[:, :hidden], down_own[...])
            + times(act_ref[:, hidden:], down_other[...])
        )

    @pl.when(step >= side)
    def _():
        put(
            times(dgate_ref[:, :hidden], pair_own[:, :hidden])
            + times(dup_ref[:, :hidden], pair_own[:, hidden:])
            + times(dgate_ref[:, hidden:], pair_other[:, :hidden])
            + times(dup_ref[:, hidden:], pair_other[:, hidden:])
        )


def expert_out(half_of, act, dgate, dup, own, other, pieces, added=None):
    count = act.shape[0] // 2
    width, hidden = own[1].shape
    tile = 2 * TILE
    side = width // tile
    whole = pl.BlockSpec((count, 2 * hidden), lambda n: (half_of, 0))
    wide = pl.BlockSpec((count, tile), lambda n: (0, n))
    down_spec = pl.BlockSpec((tile, hidden), lambda n: (jnp.minimum(n, side - 1), 0))
    pair_spec = pl.BlockSpec((tile, 2 * hidden), lambda n: (jnp.clip(n - side, 0, side - 1), 0))
    in_specs = [whole] * 3 + [down_spec, pair_spec] * 2
    operands = [act, dgate, dup, own[1], own[0], other[1], other[0]]
    if added is not None:
        in_specs.append(wide)
        operands.append(added)
    rows = count // pieces
    return pl.pallas_call(
        functools.partial(expert_out_kernel, added is not None),
        out_shape=[jax.ShapeDtypeStruct((rows, 2 * width), jnp.bfloat16)] * pieces,
        grid=(2 * side,),
        in_specs=in_specs,
        out_specs=[pl.BlockSpec((rows, tile), lambda n: (0, n))] * pieces,
        cost_estimate=pl.CostEstimate(
            flops=12 * count * width * hidden,
            bytes_accessed=12 * width * hidden + 8 * count * width,
            transcendentals=0,
        ),
    )(*operands)


def join_halves(mine, other, first_is_mine):
    top = jnp.where(first_is_mine, mine, other)
    bottom = jnp.where(first_is_mine, other, mine)
    return jnp.concatenate([top, bottom], axis=0)


def split_three(values_in):
    high = values_in.astype(jnp.bfloat16)
    rest = values_in - high.astype(jnp.float32)
    middle = rest.astype(jnp.bfloat16)
    low = (rest - middle.astype(jnp.float32)).astype(jnp.bfloat16)
    return [high, middle, low]


def local(
    layer_in,
    w_qkv,
    w_out,
    norm_gains,
    router,
    w_gate_up,
    w_down,
    routes,
    lengths,
    token_order,
    out_grad,
):
    bf16, f32 = jnp.bfloat16, jnp.float32
    highest = lax.Precision.HIGHEST
    tokens, width = layer_in.shape
    experts = router.shape[1]
    hidden = w_down.shape[2]
    half = tokens // 2
    owners = OWNERS
    tp_index = lax.axis_index(TP)
    ctx_index = lax.axis_index(CTX)
    ctx_size = lax.axis_size(CTX)
    expert_index = lax.axis_index(SHARD) * ctx_size + ctx_index
    first_is_mine = tp_index == 0
    my_row = tp_index * half
    other_row = (1 - tp_index) * half

    def my_rows(values_in):
        return lax.dynamic_slice_in_dim(values_in, my_row, half)

    def other_rows(values_in):
        return lax.dynamic_slice_in_dim(values_in, other_row, half)

    small_all = lax.all_gather(
        jnp.concatenate([norm_gains, router], axis=1), owners, axis=0, tiled=True
    )
    qkv_all = lax.all_gather(w_qkv, owners, axis=0, tiled=True)
    out_all = lax.all_gather(w_out, owners, axis=0, tiled=True)
    grad_half = my_rows(out_grad)
    shards = lax.axis_size(SHARD)
    shard_index = lax.axis_index(SHARD)
    steps = range(shards)

    def gather_groups(block):
        near_blocks = [block] + [shift_shard(block, step) for step in steps[1:]]
        far_blocks = [swap_ctx(block, 2) for block in near_blocks]
        near_group = row_major(jnp.concatenate(near_blocks, axis=0))
        far_group = row_major(jnp.concatenate(far_blocks, axis=0))
        return [
            [near_group, swap_ctx(near_group, 1)],
            [far_group, swap_ctx(far_group, 1)],
        ]

    grad_groups = gather_groups(grad_half)
    pair_own = jnp.concatenate([w_gate_up[0, :, 0], w_gate_up[0, :, 1]], axis=1)
    pair_other = swap_tp(pair_own)

    def hidden_part(which, index):
        return which[:, index * hidden : (index + 1) * hidden]

    half_width = qkv_all.shape[1]
    full_heads = half_width * lax.axis_size(TP)
    head_count = half_width // HEAD
    gains_f = small_all[:, :4].astype(f32)
    router_f = small_all[:, 4:].astype(f32)
    gain_in = gains_f[:, 0]
    gain_mid = gains_f[:, 1]
    gain_q = lax.dynamic_slice_in_dim(gains_f[:, 2], tp_index * half_width, half_width)
    gain_k = lax.dynamic_slice_in_dim(gains_f[:, 3], tp_index * half_width, half_width)
    score_scale = HEAD ** (-0.5)
    seq_all, pos_all = places_info(token_order[0], lengths[0])

    def ctx_rows(table, index):
        return lax.dynamic_slice_in_dim(table, index * tokens, tokens)

    seq_mine, pos_mine = ctx_rows(seq_all, ctx_index), ctx_rows(pos_all, ctx_index)
    key_order = [ctx_index ^ step for step in range(ctx_size)]
    seq_keys = jnp.concatenate([ctx_rows(seq_all, i) for i in key_order])
    pos_keys = jnp.concatenate([ctx_rows(pos_all, i) for i in key_order])
    cosine, sine = rope_tables(pos_mine, HEAD)
    visible = (seq_mine[:, None] == seq_keys[None, :]) & (pos_keys[None, :] <= pos_mine[:, None])

    layer_f = layer_in.astype(f32)
    rate_in = lax.rsqrt(jnp.mean(layer_f * layer_f, axis=-1, keepdims=True) + norm_eps)
    in_hat = layer_f * rate_in
    in_low = row_major((in_hat * gain_in).astype(bf16))
    qkv_mats = qkv_all.reshape(3, width, half_width)
    q_raw, k_raw, v_raw = (
        jnp.dot(in_low, qkv_mats[j], preferred_element_type=f32) for j in range(3)
    )
    v_low = v_raw.astype(bf16)
    square_q, square_k = lax.psum(
        (jnp.sum(q_raw * q_raw, axis=1), jnp.sum(k_raw * k_raw, axis=1)), TP
    )
    down_own = lax.optimization_barrier((w_down[0], square_q))[0]
    down_other = swap_tp(down_own)
    own_weights, other_weights = (pair_own, w_down[0]), (pair_other, down_other)
    rate_q = lax.rsqrt(square_q / full_heads + norm_eps)[:, None]
    rate_k = lax.rsqrt(square_k / full_heads + norm_eps)[:, None]
    q_hat = q_raw * rate_q
    k_hat = k_raw * rate_k
    q_low = rotate((q_hat * gain_q).reshape(tokens, head_count, HEAD), cosine, sine).astype(bf16)
    k_low = (
        rotate((k_hat * gain_k).reshape(tokens, head_count, HEAD), cosine, sine)
        .astype(bf16)
        .reshape(tokens, half_width)
    )

    def gather_ctx(block):
        far = swap_ctx(block, 2)
        return jnp.concatenate([block, swap_ctx(block, 1), far, swap_ctx(far, 1)], axis=0)

    group_len = tokens * ctx_size
    value_heads = gather_ctx(v_low).reshape(group_len, head_count, HEAD)
    key_heads = gather_ctx(k_low).reshape(group_len, head_count, HEAD)
    scores = jnp.einsum("qhd,khd->hqk", q_low, key_heads, preferred_element_type=f32) * score_scale
    scores = jnp.where(visible[None], scores, masked_score)
    row_max = jnp.max(scores, axis=-1, keepdims=True)
    shifted = jnp.exp(scores - row_max)
    row_sum = jnp.sum(shifted, axis=-1, keepdims=True)
    weights = shifted / row_sum
    log_total = row_max + jnp.log(row_sum)
    mixed = jnp.einsum(
        "hqk,khd->qhd", weights.astype(bf16), value_heads, preferred_element_type=f32
    )
    mixed_low = mixed.reshape(tokens, half_width).astype(bf16)
    attn_part = lax.dot_general(
        mixed_low, out_all, (((1,), (1,)), ((), ())), preferred_element_type=f32
    )
    attn_part = row_major(attn_part)
    attn = my_rows(attn_part) + swap_tp(other_rows(attn_part).astype(bf16)).astype(f32)

    resid = my_rows(layer_f) + attn
    rate_mid = lax.rsqrt(jnp.mean(resid * resid, axis=-1, keepdims=True) + norm_eps)
    mid_hat = resid * rate_mid
    mid_norm = mid_hat * gain_mid
    logits = jnp.dot(mid_norm, router_f, precision=highest)
    expert_ids = jnp.arange(experts, dtype=jnp.int32)
    chosen = jnp.any(my_rows(routes)[:, :, None] == expert_ids[None, None, :], axis=1)
    logits_max = jnp.max(jnp.where(chosen, logits, -jnp.inf), axis=-1, keepdims=True)
    gates = jnp.where(chosen, jnp.exp(jnp.where(chosen, logits - logits_max, 0.0)), 0.0)
    gates = gates / jnp.sum(gates, axis=-1, keepdims=True)

    def padded(parts):
        columns = sum(part.shape[1] for part in parts)
        rest = -columns % LANES
        if rest:
            parts = parts + [jnp.zeros((parts[0].shape[0], rest), parts[0].dtype)]
        return jnp.concatenate(parts, axis=1)

    mid_groups = gather_groups(row_major(padded([mid_norm.astype(bf16)] + split_three(gates))))
    index = expert_index.astype(jnp.int32).reshape(1)
    inside = [
        expert_in(index, mid_groups[far], grad_groups[far], own_weights, other_weights, experts)
        for far in range(2)
    ]

    def send_side(far):
        sent = expert_out(1, *inside[far][:3], own_weights, other_weights, 1)[0]
        return swap_ctx(sent, 1)

    def sum_side(far, arrived):
        return expert_out(0, *inside[far][:3], own_weights, other_weights, shards, arrived)

    arrived_sides = [send_side(1), send_side(0)]
    far_sums = sum_side(1, arrived_sides[0])
    far_arrived = [swap_ctx(far_sums[step], 2) for step in steps]
    near_sums = sum_side(0, arrived_sides[1])
    block_sums = [add_low(mine, other) for mine, other in zip(near_sums, far_arrived)]
    step_arrived = [
        shift_shard(block_sums[step].astype(bf16), -step) for step in steps[1:]
    ]
    block_total = row_major(add_low(block_sums[0], *step_arrived))

    pairs = [(far, side) for far in range(2) for side in range(2)]
    mid_all = jnp.concatenate([mid_groups[far][side] for far, side in pairs], axis=0)[:, :width]
    act_all, dgate_all, dup_all = (
        jnp.concatenate([inside[far][which] for far in range(2)], axis=0) for which in range(3)
    )
    grad_all = jnp.concatenate([grad_groups[far][side] for far, side in pairs], axis=0)

    def over_tokens(rows, columns):
        return lax.dot_general(
            rows, columns, (((0,), (0,)), ((), ())), preferred_element_type=f32
        )

    pair_rows = jnp.concatenate(
        [hidden_part(dgate_all, 1), hidden_part(dup_all, 1)], axis=1
    )
    pair_sent = over_tokens(mid_all, pair_rows).astype(bf16)
    pair_arrived = swap_tp(pair_sent)
    gate_up_grad = jnp.stack(
        [
            over_tokens(mid_all, hidden_part(which, 0))
            + hidden_part(pair_arrived, position).astype(f32)
            for position, which in enumerate((dgate_all, dup_all))
        ],
        axis=1,
    )[None]
    down_sent = over_tokens(grad_all, hidden_part(act_all, 1)).astype(bf16)

    score_rel = jnp.concatenate([jnp.sum(inside[far][3], axis=1) for far in range(2)], axis=0)
    blocks = jnp.arange(shards * ctx_size, dtype=jnp.int32)
    place = (ctx_index ^ (blocks % ctx_size)) * shards + (
        shard_index + shards - blocks // ctx_size
    ) % shards
    score_abs = jnp.take(score_rel.reshape(-1, half), place, axis=0)
    score_total = lax.all_to_all(
        score_abs, owners, split_axis=0, concat_axis=0, tiled=True
    ).T

    mixture = block_total[:, :width]
    mid_grad = block_total[:, width : 2 * width]
    output_half = (resid + mixture).astype(bf16)
    output_other = swap_tp(output_half)
    output = join_halves(output_half, output_other, first_is_mine)
    logit_grad = gates * (score_total - jnp.sum(gates * score_total, axis=1, keepdims=True))
    router_grad = lax.dot_general(
        logit_grad, mid_norm, (((0,), (0,)), ((), ())), precision=highest
    )
    mid_grad = mid_grad + lax.dot_general(
        logit_grad, router_f, (((1,), (1,)), ((), ())), precision=highest
    )
    mid_scaled = gain_mid * mid_grad
    resid_grad = grad_half.astype(f32) + rate_mid * (
        mid_scaled - mid_hat * jnp.mean(mid_hat * mid_scaled, axis=-1, keepdims=True)
    )
    gain_mid_grad = jnp.sum(mid_grad * mid_hat, axis=0, keepdims=True)
    attn_half = resid_grad.astype(bf16)
    attn_low = join_halves(attn_half, swap_tp(attn_half), first_is_mine)
    out_proj_grad = lax.dot_general(
        attn_low, mixed_low, (((0,), (0,)), ((), ())), preferred_element_type=f32
    ).astype(bf16)
    out_owned = lax.psum_scatter(out_proj_grad, owners, scatter_dimension=0, tiled=True)
    out_owned = out_owned.astype(f32)
    mixed_grad = (
        jnp.dot(attn_low, out_all, preferred_element_type=f32)
        .astype(bf16)
        .reshape(tokens, head_count, HEAD)
    )
    again = jnp.einsum("qhd,khd->hqk", q_low, key_heads, preferred_element_type=f32) * score_scale
    again = jnp.where(visible[None], again, masked_score)
    weights_again = jnp.exp(again - log_total)
    weights_low = weights_again.astype(bf16)
    weight_grad = jnp.einsum("qhd,khd->hqk", mixed_grad, value_heads, preferred_element_type=f32)
    score_grad = weights_again * (
        weight_grad - jnp.sum(weights_again * weight_grad, axis=-1, keepdims=True)
    )
    score_low = score_grad.astype(bf16)
    q_grad = (
        jnp.einsum("hqk,khd->qhd", score_low, key_heads, preferred_element_type=f32) * score_scale
    )
    k_part = (
        jnp.einsum("hqk,qhd->khd", score_low, q_low, preferred_element_type=f32) * score_scale
    )
    v_part = jnp.einsum("hqk,qhd->khd", weights_low, mixed_grad, preferred_element_type=f32)

    kv_part = jnp.concatenate(
        [
            part.reshape(ctx_size, tokens, half_width).astype(bf16)
            for part in (k_part, v_part)
        ],
        axis=2,
    )
    kv_arrived = swap_ctx(jnp.stack([kv_part[1], kv_part[3]]), 1)
    kv_far = add_low(kv_part[2], kv_arrived[1]).astype(bf16)
    kv_grad = add_low(kv_part[0], kv_arrived[0], swap_ctx(kv_far, 2))
    k_grad, v_grad = kv_grad[:, :half_width], kv_grad[:, half_width:]
    q_in = rotate_back(q_grad, cosine, sine).reshape(tokens, half_width)
    k_in = rotate_back(k_grad.reshape(tokens, head_count, HEAD), cosine, sine).reshape(
        tokens, half_width
    )
    q_scaled = gain_q * q_in
    k_scaled = gain_k * k_in
    inner_q, inner_k = lax.psum(
        (jnp.sum(q_scaled * q_hat, axis=1), jnp.sum(k_scaled * k_hat, axis=1)), TP
    )
    down_sent = lax.optimization_barrier((down_sent, inner_q))[0]
    down_arrived = swap_tp(down_sent)
    down_grad = (over_tokens(grad_all, hidden_part(act_all, 0)) + down_arrived.astype(f32))[None]
    q_raw_grad = rate_q * (q_scaled - q_hat * (inner_q / full_heads)[:, None])
    k_raw_grad = rate_k * (k_scaled - k_hat * (inner_k / full_heads)[:, None])
    raw_grads = [q_raw_grad.astype(bf16), k_raw_grad.astype(bf16), v_grad.astype(bf16)]
    raw_stack = jnp.stack(raw_grads)
    in_turned = in_low.T
    block_rows = w_qkv.shape[0]

    def grad_blocks(far, side, added=None):
        order = jnp.stack(
            [
                ((shard_index + step) % shards) * ctx_size + (ctx_index ^ (2 * far + side))
                for step in steps
            ]
        ).astype(jnp.int32)
        return weight_grad_blocks(order, in_turned, raw_stack, block_rows, added)

    far_grads = grad_blocks(1, 0, swap_ctx(grad_blocks(1, 1), 1))
    far_grads_in = [swap_ctx(far_grads[step], 2) for step in steps]
    near_grads = grad_blocks(0, 0, swap_ctx(grad_blocks(0, 1), 1))
    step_grads = [add_low(near_grads[step], far_grads_in[step]) for step in steps]
    step_grads_in = [shift_shard(step_grads[step].astype(bf16), step) for step in steps[1:]]
    qkv_owned = add_low(step_grads[0], *step_grads_in)
    norm_part = sum(
        lax.dot_general(raw, mat, (((1,), (1,)), ((), ())), preferred_element_type=f32)
        for raw, mat in zip(raw_grads, (qkv_mats[0], qkv_mats[1], qkv_mats[2]))
    )
    norm_arrived = swap_tp(other_rows(norm_part).astype(bf16))
    in_norm_grad = my_rows(norm_part) + norm_arrived.astype(f32)
    in_hat_half = my_rows(in_hat)
    in_scaled = gain_in * in_norm_grad
    input_half = resid_grad + my_rows(rate_in) * (
        in_scaled - in_hat_half * jnp.mean(in_hat_half * in_scaled, axis=-1, keepdims=True)
    )
    input_grad = join_halves(input_half, swap_tp(input_half), first_is_mine)
    gain_in_grad = jnp.sum(in_norm_grad * in_hat_half, axis=0, keepdims=True)
    gain_pair = jnp.stack([jnp.sum(q_in * q_hat, axis=0), jnp.sum(k_in * k_hat, axis=0)], axis=0)
    qk_gain_part = lax.dynamic_update_slice(
        jnp.zeros((2, width), f32), gain_pair, (0, tp_index * half_width)
    )
    early_total = lax.psum(jnp.concatenate([router_grad, gain_mid_grad], axis=0), (SHARD, CTX, TP))
    late = jnp.concatenate([gain_in_grad, qk_gain_part], axis=0)
    late = late + swap_tp(late)
    late = late + swap_ctx(late, 1)
    late = late + swap_ctx(late, 2)
    late_total = late + sum(shift_shard(late, step) for step in steps[1:])

    def owned(total):
        count = norm_gains.shape[0]
        return lax.dynamic_slice_in_dim(total, expert_index * count, count, axis=1)

    gains_total = jnp.concatenate([late_total[:1], early_total[experts:], late_total[1:]], axis=0)
    gains_owned = owned(gains_total).T
    router_owned = owned(early_total[:experts]).T

    return (
        output,
        input_grad,
        qkv_owned,
        out_owned,
        gains_owned,
        router_owned,
        gate_up_grad,
        down_grad,
    )


def solution(mesh):
    in_specs = (
        P(OWNERS, None),
        P(OWNERS, TP),
        P(OWNERS, TP),
        P(OWNERS, None),
        P(OWNERS, None),
        P(OWNERS, None, None, TP),
        P(OWNERS, None, TP),
        P(OWNERS, None),
        P(SHARD, None),
        P(SHARD, None),
        P(OWNERS, None),
    )
    out_specs = (
        P(OWNERS, None),
        P(OWNERS, None),
        P(OWNERS, TP),
        P(OWNERS, TP),
        P(OWNERS, None),
        P(OWNERS, None),
        P(OWNERS, None, None, TP),
        P(OWNERS, None, TP),
    )

    return jax.shard_map(local, mesh=mesh, in_specs=in_specs, out_specs=out_specs, check_vma=False)
```
